512 devices in a mesh: dp: 8 (over x, y_hi), seq: 64 (over z, y_lo, core).
Axes of the slice: x: 4, y: 8 (y_hi: 2, y_lo: 4; y = y_hi * 4 + y_lo), z: 8, core: 2. Of those that a mesh axis runs over, the one named last changes fastest.
Arguments:
- points: bfloat16 [8, 16384, 384], P('dp', 'seq'), may hold values from -6 to 6
- cotangent: bfloat16 [8, 16384, 384], P('dp', 'seq'), may hold values from -6 to 6
- in_gain: float32 [384], replicated, may hold values from 0.5 to 2
- out_gain: float32 [384], replicated, may hold values from 0.5 to 2
- left_factor: bfloat16 [256, 256], replicated, may hold values from -0.375 to 0.375
- right_factor: bfloat16 [64, 64], replicated, may hold values from -0.75 to 0.75
- norm_gain: float32 [384], replicated, may hold values from 0.5 to 2
- gate_weight: bfloat16 [4, 96, 384], P(None, None, 'dp'), may hold values from -0.625 to 0.625
- up_weight: bfloat16 [4, 96, 384], P(None, None, 'dp'), may hold values from -0.625 to 0.625
- down_weight: bfloat16 [4, 96, 384], P(None, None, 'dp'), may hold values from -0.3125 to 0.3125
Outputs:
- layer_out: bfloat16 [8, 16384, 384], P('dp', 'seq')
- grad_points: bfloat16 [8, 16384, 384], P('dp', 'seq')
- grad_left: float32 [256, 256], replicated
- grad_right: float32 [64, 64], replicated
- grad_in_gain: float32 [384], replicated
- grad_out_gain: float32 [384], replicated
- grad_norm_gain: float32 [384], replicated
- grad_gate: float32 [4, 96, 384], P(None, None, 'dp')
- grad_up: float32 [4, 96, 384], P(None, None, 'dp')
- grad_down: float32 [4, 96, 384], P(None, None, 'dp')
The draws below stay inside these ranges and needn't reach their ends.
All inputs are finite; a program needn't handle non-finite values.
Results may differ from the reference program's by a relative error of at most 0.0091.
Values may be sent and summed in bfloat16 or wider, within the bound.
A program may use at most 64 MiB of HBM per device.

```python
import math
import jax
import jax.numpy as jnp
from jax import lax

D = 384
NBC = 4
MB = 256
NB = 64
SEQ = 16384
DESIGNS = 8
DB = 96
FB = 384
FQ = 96


def level_of(stream_key, shape, shards, low, high):
    def one(axis_at, parts):
        heights = jax.random.uniform(jax.random.fold_in(jax.random.fold_in(stream_key, 6), axis_at), (parts,), jnp.float32, low / len(shards), high / len(shards))
        return jnp.repeat(jnp.exp(heights), shape[axis_at] // parts).reshape((-1,) + (1,) * (len(shape) - axis_at - 1))

    loudness = one(*shards[0])
    for cut in shards[1:]:
        loudness = loudness * one(*cut)
    return loudness


def normal_values(stream_key, shape, width, reach, split=(), kind=jnp.bfloat16):
    array = width * jax.random.normal(stream_key, shape, jnp.float32)
    if split:
        array = array * level_of(stream_key, shape, split, -0.22, 0.18)
    return jnp.clip(array, -reach, reach).astype(kind)


def setup_inputs(seed: int = 0) -> dict:
    arg_keys = jax.random.split(jax.random.key(seed), 11)
    points = normal_values(arg_keys[0], (DESIGNS, SEQ, D), 1.0, 6.0, ((0, 8), (1, 64)))
    cotangent = normal_values(arg_keys[1], (DESIGNS, SEQ, D), 1.0, 6.0, ((0, 8), (1, 64)))
    in_gain = jnp.clip(jnp.exp(jax.random.uniform(arg_keys[2], (D,), jnp.float32, math.log(0.5), math.log(2.0))), 0.5, 2.0)
    out_gain = jnp.clip(jnp.exp(jax.random.uniform(arg_keys[3], (D,), jnp.float32, math.log(0.5), math.log(2.0))), 0.5, 2.0)
    left_factor = normal_values(arg_keys[4], (MB, MB), MB ** -0.5, 0.375)
    right_factor = normal_values(arg_keys[5], (NB, NB), NB ** -0.5, 0.75)
    norm_gain = jnp.clip(jnp.exp(jax.random.uniform(arg_keys[6], (D,), jnp.float32, math.log(0.5), math.log(2.0))), 0.5, 2.0)
    gate_weight = normal_values(arg_keys[7], (NBC, DB, FB), DB ** -0.5, 0.625, ((2, 8),))
    up_weight = normal_values(arg_keys[8], (NBC, DB, FB), DB ** -0.5, 0.625, ((2, 8),))
    down_weight = normal_values(arg_keys[9], (NBC, DB, FB), FB ** -0.5, 0.3125, ((2, 8),))
    return {"points": points, "cotangent": cotangent, "in_gain": in_gain, "out_gain": out_gain, "left_factor": left_factor, "right_factor": right_factor, "norm_gain": norm_gain, "gate_weight": gate_weight, "up_weight": up_weight, "down_weight": down_weight}


def design(inputs, cotangent, in_gain, out_gain, left_factor, right_factor, norm_gain, gate_weight, up_weight, down_weight):
    points = inputs.astype(jnp.float32)
    scaled = (points * in_gain).astype(jnp.bfloat16).reshape(NB, MB, D)
    first_mix = jnp.einsum('pb,abc->apc', left_factor.astype(jnp.float32), scaled.astype(jnp.float32)).astype(jnp.bfloat16)
    mixed = jnp.einsum('qa,apc->pqc', right_factor.astype(jnp.float32), first_mix.astype(jnp.float32)).reshape(SEQ, D)
    residual = points + out_gain * mixed
    inv_rms = lax.rsqrt(lax.optimization_barrier(jnp.mean(residual * residual, axis=-1, keepdims=True)) + 1e-05)
    normed = residual * inv_rms
    hidden_in = (normed * norm_gain).astype(jnp.bfloat16).reshape(SEQ, NBC, DB)
    hidden_f = hidden_in.astype(jnp.float32)
    gate_pre = jnp.einsum('rkd,kdf->rkf', hidden_f, gate_weight.astype(jnp.float32))
    up_pre = jnp.einsum('rkd,kdf->rkf', hidden_f, up_weight.astype(jnp.float32))
    sig_gate = jax.nn.sigmoid(gate_pre)
    act_gate = gate_pre * sig_gate
    hidden = (act_gate * up_pre).astype(jnp.bfloat16)
    hidden_grid = hidden.astype(jnp.float32).reshape(SEQ, NBC, NBC, FQ)
    down_grid = down_weight.astype(jnp.float32).reshape(NBC, DB, NBC, FQ)
    branch = jnp.einsum('rkjf,jokf->rjo', hidden_grid, down_grid).reshape(SEQ, D)
    layer_out = (residual + branch).astype(jnp.bfloat16)
    grad_f = cotangent.astype(jnp.float32)
    grad_grid = grad_f.reshape(SEQ, NBC, DB)
    dhidden = jnp.einsum('rjo,jokf->rkjf', grad_grid, down_grid).reshape(SEQ, NBC, FB)
    grad_down = jnp.einsum('rjo,rkjf->jokf', grad_grid, hidden_grid).reshape(NBC, DB, FB)
    dgate = (dhidden * up_pre * sig_gate * (1.0 + gate_pre * (1.0 - sig_gate))).astype(jnp.bfloat16).astype(jnp.float32)
    dup = (dhidden * act_gate).astype(jnp.bfloat16).astype(jnp.float32)
    dhid_in = jnp.einsum('rkf,kdf->rkd', dgate, gate_weight.astype(jnp.float32))
    dhid_in = (dhid_in + jnp.einsum('rkf,kdf->rkd', dup, up_weight.astype(jnp.float32))).reshape(SEQ, D)
    grad_gate = jnp.einsum('rkd,rkf->kdf', hidden_f, dgate)
    grad_up = jnp.einsum('rkd,rkf->kdf', hidden_f, dup)
    grad_norm = lax.optimization_barrier(jnp.sum(dhid_in * normed, axis=0))
    scaled_grad = dhid_in * norm_gain
    dresid = grad_f + inv_rms * (scaled_grad - normed * lax.optimization_barrier(jnp.mean(scaled_grad * normed, axis=-1, keepdims=True)))
    grad_out = lax.optimization_barrier(jnp.sum(dresid * mixed, axis=0))
    dmixed = (dresid * out_gain).astype(jnp.bfloat16).astype(jnp.float32).reshape(MB, NB, D)
    dfirst = jnp.einsum('qa,pqc->apc', right_factor.astype(jnp.float32), dmixed).astype(jnp.bfloat16).astype(jnp.float32)
    grad_right = jnp.einsum('pqc,apc->qa', dmixed, first_mix.astype(jnp.float32))
    dscaled = jnp.einsum('pb,apc->abc', left_factor.astype(jnp.float32), dfirst)
    grad_left = jnp.einsum('apc,abc->pb', dfirst, scaled.astype(jnp.float32))
    dscaled = dscaled.reshape(SEQ, D)
    grad_in = lax.optimization_barrier(jnp.sum(dscaled * points, axis=0))
    grad_points = (dresid + dscaled * in_gain).astype(jnp.bfloat16)
    return (layer_out, grad_points, grad_left, grad_right, grad_in, grad_out, grad_norm, grad_gate, grad_up, grad_down)

def reference(points, cotangent, in_gain, out_gain, left_factor, right_factor, norm_gain, gate_weight, up_weight, down_weight):

    def per_design(inputs_pair):
        return design(inputs_pair[0], inputs_pair[1], in_gain, out_gain, left_factor, right_factor, norm_gain, gate_weight, up_weight, down_weight)
    results = lax.map(per_design, (points, cotangent))
    factor = float(DESIGNS * SEQ) ** (-0.5)
    summed = [lax.optimization_barrier(jnp.sum(item, axis=0)) * factor for item in results[2:]]
    return (results[0], results[1], summed[0], summed[1], summed[2], summed[3], summed[4], summed[5], summed[6], summed[7])
```

```python
import functools

import jax
import jax.numpy as jnp
from jax import lax
from jax.experimental import pallas as pl
from jax.experimental.pallas import tpu as pltpu
from jax.sharding import PartitionSpec as P

MESH = pl.DeviceIdType.MESH
SLOT = 96
REP = 80


def place():
    d = lax.axis_index("dp")
    s = lax.axis_index("seq")
    return d // 2, d % 2, s // 8, (s // 2) % 4, s % 2


def device(x, yh, z, yl, c):
    return (x * 2 + yh, (z * 4 + yl) * 2 + c)


def greet(peers):
    barrier = pltpu.get_barrier_semaphore()
    for peer in peers:
        pl.semaphore_signal(barrier, inc=1, device_id=peer, device_id_type=MESH)
    pl.semaphore_wait(barrier, len(peers))


def gather_kernel(w_ref, out_ref, local_sem, send_sem, recv_sem):
    x, yh, z, yl, c = place()
    pair = device(x, yh, z, yl, 1 - c)
    xs = [device((x + k) % 4, yh, z, yl, c) for k in (1, 2, 3)]
    across = [device(x, 1 - yh, z, k, c) for k in range(4)]
    width = w_ref.shape[1]
    half = w_ref.shape[0] // 2

    def part(d):
        at = pl.ds(pl.multiple_of(d * width, 16), width)
        return out_ref.at[pl.ds(half * c, half), at, :]

    def remote(src, dst, sent, got, peer):
        return pltpu.make_async_remote_copy(
            src, dst, send_sem.at[sent], recv_sem.at[got], device_id=peer, device_id_type=MESH
        )

    greet([pair] + xs + across)
    own = w_ref.at[pl.ds(half * c, half)]
    mine = part(x * 2 + yh)
    theirs = part(x * 2 + 1 - yh)
    end = (yl == 0) | (yl == 3)
    base = 2 - 2 * (yl // 3)
    over = [
        remote(own, mine, n, 0, device(x, 1 - yh, z, base + n, c)) for n in range(2)
    ]

    @pl.when(end)
    def _():
        for copy in over:
            copy.start()

    local = pltpu.make_async_copy(own, mine, local_sem)
    local.start()
    sends = [remote(own, mine, 2 + n, 1 + n, peer) for n, peer in enumerate(xs)]
    for copy in sends:
        copy.start()
    over[0].wait_recv()
    for n, peer in enumerate(xs):
        copy = remote(theirs, theirs, 5 + n, 4 + n, peer)
        copy.start()
        sends.append(copy)
    local.wait()
    for copy in sends:
        copy.wait_recv()
    whole = out_ref.at[pl.ds(half * c, half)]
    copy = remote(whole, whole, 8, 7, pair)
    copy.start()
    copy.wait_recv()
    for copy in sends + [copy]:
        copy.wait_send()

    @pl.when(end)
    def _():
        for copy in over:
            copy.wait_send()


def gather_weights(w):
    n, width, d = w.shape
    return pl.pallas_call(
        gather_kernel,
        out_shape=jax.ShapeDtypeStruct((n, 8 * width, d), w.dtype),
        in_specs=[pl.BlockSpec(memory_space=pltpu.VMEM)],
        out_specs=pl.BlockSpec(memory_space=pltpu.VMEM),
        scratch_shapes=[
            pltpu.SemaphoreType.DMA,
            pltpu.SemaphoreType.DMA((9,)),
            pltpu.SemaphoreType.DMA((8,)),
        ],
        compiler_params=pltpu.CompilerParams(collective_id=1, has_side_effects=True),
        cost_estimate=pl.CostEstimate(flops=0, bytes_accessed=40_000_000, transcendentals=0),
        name="gather_weights",
    )(w)


PIECES = (
    ((0, 0, 0, 48),),
    ((0, 48, 0, 32), (1, 0, 32, 16)),
    ((1, 16, 0, 48),),
    ((2, 0, 0, 48),),
    ((2, 48, 0, 32), (3, 0, 32, 16)),
    ((3, 16, 0, 48),),
)


def sum_kernel(
    factor,
    gate_ref, up_ref, down_ref, left_ref, right_ref, in_ref, outg_ref, norm_ref,
    out_ref,
    rep_ref, wgot, rgot, xsend, xgot, ysend, ygot, zall, yall, wother, repall,
    send_sem, recv_sem,
):
    x, yh, z, yl, c = place()
    f32, bf16 = jnp.float32, jnp.bfloat16
    y = yh * 4 + yl
    pair = device(x, yh, z, yl, 1 - c)
    xs = [device((x + k) % 4, yh, z, yl, c) for k in (1, 2, 3)]
    xo = [device((x + k) % 4, yh, z, yl, 1 - c) for k in (1, 2, 3)]
    near = [device(x, yh, z, (yl + k) % 4, c) for k in (1, 2, 3)]
    far = [device(x, 1 - yh, z, (yl + k) % 4, c) for k in (0, 1, 2, 3)]
    zs = [device(x, yh, (z + k) % 8, yl, c) for k in range(1, 8)]
    greet([pair] + xs + xo + near + far + zs)
    started = []

    def send(src, dst, peer):
        n = len(started)
        copy = pltpu.make_async_remote_copy(
            src, dst, send_sem.at[n], recv_sem.at[n], device_id=peer, device_id_type=MESH
        )
        copy.start()
        started.append(copy)
        return copy

    def landed(copies):
        for copy in copies:
            copy.wait_recv()

    grads = (gate_ref, up_ref, down_ref)
    copies = [
        send(ref.at[pl.ds(2 * (1 - c), 2)], wgot.at[kind], pair)
        for kind, ref in enumerate(grads)
    ]
    for k in range(4):
        for n in range(8):
            row, lane = (k % 2) * 128 + n * 16, (k // 2) * 128
            rep_ref[0, k, n] = left_ref[row : row + 16, lane : lane + 128].astype(bf16)
            rep_ref[1, k, n] = jnp.zeros((16, 128), bf16)
    for n in range(2):
        for j in range(2):
            at = slice(32 * j + 16 * n, 32 * j + 16 * n + 16)
            rep_ref[1, 0, n, :, 64 * j : 64 * j + 64] = right_ref[at, :].astype(bf16)
    gains = [
        ref[128 * t : 128 * t + 128].reshape(1, 128)
        for ref in (in_ref, outg_ref, norm_ref)
        for t in range(3)
    ]
    gains.append(jnp.zeros((7, 128), f32))
    rep_ref[1, 0, 2] = jnp.concatenate(gains, axis=0).astype(bf16)
    copies.append(send(rep_ref.at[1 - c], rgot, pair))
    for dest in range(4):
        for h in range(2):
            for q in range(4):
                xsend[dest, h * 4 + q, 0:REP, 96:128] = jnp.zeros((REP, 32), bf16)
            for q in (1, 3):
                xsend[dest, h * 4 + q, 64:REP] = jnp.zeros((REP - 64, 128), bf16)
    landed(copies)
    for dest in range(4):
        for h in range(2):
            first = (dest * 2 + h) * 48
            for i, pieces in enumerate(PIECES):
                kind, k = divmod(i, 2)
                for q, row, start, rows in pieces:
                    at = slice(first + start, first + start + rows)
                    total = grads[kind][2 * c + k, at, :].astype(f32)
                    total = total + wgot[kind, k, at, :].astype(f32)
                    xsend[dest, h * 4 + q, row : row + rows, 0:96] = total.astype(bf16)
        total = rep_ref[c, dest].astype(f32) + rgot[dest].astype(f32)
        xsend[dest, :, REP:SLOT, :] = total.astype(bf16)

    copies = [
        send(xsend.at[(x + k) % 4], xgot.at[k - 1], peer) for k, peer in zip((1, 2, 3), xs)
    ]
    landed(copies)

    def add_x(n, carry):
        total = xsend[x, n].astype(f32)
        for k in range(3):
            total = total + xgot[k, n].astype(f32)
        ysend[n] = total.astype(bf16)
        return carry

    lax.fori_loop(0, 8, add_x, 0)

    copies = [
        send(ysend.at[yh * 4 + (yl + k) % 4], ygot.at[k - 1], peer)
        for k, peer in zip((1, 2, 3), near)
    ]
    copies += [
        send(ysend.at[(1 - yh) * 4 + (yl + k) % 4], ygot.at[3 + k], peer)
        for k, peer in zip((0, 1, 2, 3), far)
    ]
    landed(copies)
    total = ysend[y].astype(f32)
    for k in range(7):
        total = total + ygot[k].astype(f32)
    zall[z] = total.astype(bf16)

    landed([send(zall.at[z], zall.at[z], peer) for peer in zs])
    total = zall[0].astype(f32)
    for k in range(1, 8):
        total = total + zall[k].astype(f32)
    yall[y] = total.astype(bf16)

    copies = [send(yall.at[y], yall.at[y], peer) for peer in near]
    tail = yall.at[y, REP:SLOT]
    copies += [send(tail, tail, peer) for peer in far]
    landed(copies)
    copies = [send(yall.at[pl.ds(4 * yh, 4)], wother, pair)]
    tails = yall.at[:, REP:SLOT]
    copies += [send(tails, repall.at[c, x], peer) for peer in [pair] + xs + xo]
    repall[c, x] = yall[:, REP:SLOT, :]

    def unpack(chunk, core):
        for i, pieces in enumerate(PIECES):
            kind, k = divmod(i, 2)
            for q, row, start, rows in pieces:
                at = pl.multiple_of(kind * 192 + (2 * core + k) * 48 + start, 16)
                value = chunk(q)[row : row + rows, 0:96].astype(f32) * factor
                out_ref[pl.ds(at, rows), 256:352] = value

    unpack(lambda q: yall.at[4 * yh + q], c)
    landed(copies)
    unpack(lambda q: wother.at[q], 1 - c)
    for k in range(4):
        for n in range(8):
            row, lane = (k % 2) * 128 + n * 16, (k // 2) * 128
            value = repall[0, k, n].astype(f32) * factor
            out_ref[row : row + 16, lane : lane + 128] = value
    for n in range(2):
        value = repall[1, 0, n].astype(f32) * factor
        out_ref[256 + n * 16 : 272 + n * 16, 0:64] = value[:, 0:64]
        out_ref[288 + n * 16 : 304 + n * 16, 0:64] = value[:, 64:128]
    value = repall[1, 0, 2].astype(f32) * factor
    for j in range(3):
        for t in range(3):
            row = value[3 * j + t : 3 * j + t + 1, :]
            out_ref[576 + j : 577 + j, t * 128 : t * 128 + 128] = row
    for copy in started:
        copy.wait_send()


def sum_gradients(grads, factor):
    vmem = pl.BlockSpec(memory_space=pltpu.VMEM)
    bf16 = jnp.bfloat16
    copies = 4 + 3 + 7 + 7 + 7 + 8
    return pl.pallas_call(
        functools.partial(sum_kernel, factor),
        out_shape=jax.ShapeDtypeStruct((584, 384), jnp.float32),
        in_specs=[vmem] * len(grads),
        out_specs=vmem,
        scratch_shapes=[
            pltpu.VMEM((2, 4, 8, 16, 128), bf16),
            pltpu.VMEM((3, 2, 384, 96), bf16),
            pltpu.VMEM((4, 8, 16, 128), bf16),
            pltpu.VMEM((4, 8, SLOT, 128), bf16),
            pltpu.VMEM((3, 8, SLOT, 128), bf16),
            pltpu.VMEM((8, SLOT, 128), bf16),
            pltpu.VMEM((7, SLOT, 128), bf16),
            pltpu.VMEM((8, SLOT, 128), bf16),
            pltpu.VMEM((8, SLOT, 128), bf16),
            pltpu.VMEM((4, SLOT, 128), bf16),
            pltpu.VMEM((2, 4, 8, 16, 128), bf16),
            pltpu.SemaphoreType.DMA((copies,)),
            pltpu.SemaphoreType.DMA((copies,)),
        ],
        compiler_params=pltpu.CompilerParams(collective_id=2, has_side_effects=True),
        name="sum_gradients",
    )(*grads)


def shards(
    points,
    cotangent,
    in_gain,
    out_gain,
    left_factor,
    right_factor,
    norm_gain,
    gate_weight,
    up_weight,
    down_weight,
):
    seq_count = lax.axis_size("seq")
    data_count = lax.axis_size("dp")
    row_count = points.shape[1]
    channels = points.shape[2]
    block_size = left_factor.shape[0]
    block_total = right_factor.shape[0]
    blocks = row_count // block_size
    shard_width = gate_weight.shape[2]
    nblocks, block_in = gate_weight.shape[:2]
    block_hidden = data_count * shard_width
    quarter = block_hidden // nblocks
    packed = jnp.concatenate([gate_weight, up_weight, down_weight], axis=0).transpose(0, 2, 1)
    weights = gather_weights(packed)
    gate_full, up_full, down_full = weights[0:4], weights[4:8], weights[8:12]
    inputs = points[0].astype(jnp.float32)
    scaled = (inputs * in_gain).astype(jnp.bfloat16).reshape(blocks, block_size, channels)
    first_mix = jnp.einsum(
        "pb,abc->apc", left_factor, scaled, preferred_element_type=jnp.float32
    ).astype(jnp.bfloat16)
    received = lax.all_to_all(first_mix, "seq", split_axis=1, concat_axis=0, tiled=True)
    mixed = jnp.einsum("qa,apc->pqc", right_factor, received, preferred_element_type=jnp.float32)
    first_moved = received
    mixed = mixed.reshape(row_count, channels)
    residual = inputs + out_gain * mixed
    inv_rms = lax.rsqrt(jnp.mean(residual * residual, axis=-1, keepdims=True) + 1e-05)
    normed = residual * inv_rms
    hidden_in = (normed * norm_gain).astype(jnp.bfloat16).reshape(row_count, nblocks, block_in)
    gate_pre = jnp.einsum("rkd,kfd->rkf", hidden_in, gate_full, preferred_element_type=jnp.float32)
    up_pre = jnp.einsum("rkd,kfd->rkf", hidden_in, up_full, preferred_element_type=jnp.float32)
    sig_gate = jax.nn.sigmoid(gate_pre)
    act_gate = gate_pre * sig_gate
    hidden = (act_gate * up_pre).astype(jnp.bfloat16)
    hidden_grid = hidden.reshape(row_count, nblocks, nblocks, quarter)
    down_grid = down_full.reshape(nblocks, nblocks, quarter, block_in)
    branch = jnp.einsum(
        "rkjf,jkfo->rjo", hidden_grid, down_grid, preferred_element_type=jnp.float32
    ).reshape(row_count, channels)
    layer_out = (residual + branch).astype(jnp.bfloat16)
    grad_grid = cotangent[0].reshape(row_count, nblocks, block_in)
    dhidden = jnp.einsum(
        "rjo,jkfo->rkjf", grad_grid, down_grid, preferred_element_type=jnp.float32
    ).reshape(row_count, nblocks, block_hidden)
    grad_down = jnp.einsum(
        "rjo,rkjf->jkfo", grad_grid, hidden_grid, preferred_element_type=jnp.float32
    ).reshape(nblocks, block_hidden, block_in)
    dgate = (dhidden * up_pre * sig_gate * (1.0 + gate_pre * (1.0 - sig_gate))).astype(jnp.bfloat16)
    dupper = (dhidden * act_gate).astype(jnp.bfloat16)
    dhid_in = jnp.einsum("rkf,kfd->rkd", dgate, gate_full, preferred_element_type=jnp.float32)
    dhid_in = (
        dhid_in + jnp.einsum("rkf,kfd->rkd", dupper, up_full, preferred_element_type=jnp.float32)
    ).reshape(row_count, channels)
    grad_gate = jnp.einsum("rkd,rkf->kfd", hidden_in, dgate, preferred_element_type=jnp.float32)
    grad_up = jnp.einsum("rkd,rkf->kfd", hidden_in, dupper, preferred_element_type=jnp.float32)
    grad_norm = jnp.sum(dhid_in * normed, axis=0)
    scaled_grad = dhid_in * norm_gain
    dresid = cotangent[0].astype(jnp.float32) + inv_rms * (
        scaled_grad - normed * jnp.mean(scaled_grad * normed, axis=-1, keepdims=True)
    )
    grad_out = jnp.sum(dresid * mixed, axis=0)
    dmixed = (
        (dresid * out_gain)
        .astype(jnp.bfloat16)
        .reshape(block_size // seq_count, block_total, channels)
    )
    dfirst = jnp.einsum(
        "qa,pqc->apc", right_factor, dmixed, preferred_element_type=jnp.float32
    ).astype(jnp.bfloat16)
    grad_right = jnp.einsum("pqc,apc->qa", dmixed, first_moved, preferred_element_type=jnp.float32)
    received = lax.all_to_all(dfirst, "seq", split_axis=0, concat_axis=1, tiled=True)
    dscaled = jnp.einsum("pb,apc->abc", left_factor, received, preferred_element_type=jnp.float32)
    grad_left = jnp.einsum("apc,abc->pb", received, scaled, preferred_element_type=jnp.float32)
    dscaled = dscaled.reshape(row_count, channels)
    grad_in = jnp.sum(dscaled * inputs, axis=0)
    grad_points = (dresid + dscaled * in_gain).astype(jnp.bfloat16)
    factor = float(data_count * row_count * seq_count) ** (-0.5)
    sums = sum_gradients(
        (
            grad_gate.astype(jnp.bfloat16),
            grad_up.astype(jnp.bfloat16),
            grad_down.astype(jnp.bfloat16),
            grad_left,
            grad_right,
            grad_in,
            grad_out,
            grad_norm,
        ),
        factor,
    )

    def weight(n):
        part = sums[192 * n : 192 * n + 192, 256:352]
        return part.reshape(nblocks, shard_width, block_in).transpose(0, 2, 1)

    return (
        layer_out[None],
        grad_points[None],
        sums[0:256, 0:256],
        sums[256:320, 0:64],
        sums[576],
        sums[577],
        sums[578],
        weight(0),
        weight(1),
        weight(2),
    )


def solution(mesh):
    in_specs = (
        P("dp", "seq", None),
        P("dp", "seq", None),
        P(),
        P(),
        P(),
        P(),
        P(),
        P(None, None, "dp"),
        P(None, None, "dp"),
        P(None, None, "dp"),
    )
    out_specs = (
        P("dp", "seq", None),
        P("dp", "seq", None),
        P(),
        P(),
        P(),
        P(),
        P(),
        P(None, None, "dp"),
        P(None, None, "dp"),
        P(None, None, "dp"),
    )
    return jax.shard_map(shards, mesh=mesh, in_specs=in_specs, out_specs=out_specs, check_vma=False)
```

```python
import functools

import jax
import jax.numpy as jnp
from jax import lax
from jax.experimental import pallas as pl
from jax.experimental.pallas import tpu as pltpu
from jax.sharding import PartitionSpec as P

MESH = pl.DeviceIdType.MESH
SLOT = 96
REP = 80


def place():
    d = lax.axis_index("dp")
    s = lax.axis_index("seq")
    return d // 2, d % 2, s // 8, (s // 2) % 4, s % 2


def device(x, yh, z, yl, c):
    return (x * 2 + yh, (z * 4 + yl) * 2 + c)


def greet(peers, others=0):
    barrier = pltpu.get_barrier_semaphore()
    for peer in peers:
        pl.semaphore_signal(barrier, inc=1, device_id=peer, device_id_type=MESH)
    pl.semaphore_wait(barrier, len(peers) + others)


def line():
    d, s, n = lax.axis_index("dp"), lax.axis_index("seq"), lax.axis_size("seq")
    return d, s, n


def greet_line():
    d, s, n = line()
    barrier = pltpu.get_barrier_semaphore()

    def signal(k, carry):
        pl.semaphore_signal(
            barrier, inc=1, device_id=(d, (s + k) % n), device_id_type=MESH
        )
        return carry

    lax.fori_loop(1, n, signal, 0)
    return n - 1


class Exchange:
    def __init__(self, src, dst, local_sem, send_sem, recv_sem):
        self.refs = (src, dst)
        self.sems = (send_sem, recv_sem)
        s = lax.axis_index("seq")
        self.local = pltpu.make_async_copy(src.at[s], dst.at[s], local_sem)

    def copy(self, k):
        d, s, n = line()
        peer = (s + k) % n
        return pltpu.make_async_remote_copy(
            self.refs[0].at[peer], self.refs[1].at[s],
            self.sems[0].at[k - 1], self.sems[1].at[k - 1],
            device_id=(d, peer), device_id_type=MESH,
        )

    def start(self):
        def one(k, carry):
            self.copy(k).start()
            return carry

        lax.fori_loop(1, line()[2], one, 0)
        self.local.start()

    def wait(self):
        def one(k, carry):
            self.copy(k).wait()
            return carry

        self.local.wait()
        lax.fori_loop(1, line()[2], one, 0)


def gather_kernel(
    w_ref, mix_ref, out_ref, got_ref,
    local_sem, send_sem, recv_sem, own_sem, line_send, line_recv,
):
    x, yh, z, yl, c = place()
    pair = device(x, yh, z, yl, 1 - c)
    xs = [device((x + k) % 4, yh, z, yl, c) for k in (1, 2, 3)]
    across = [device(x, 1 - yh, z, k, c) for k in range(4)]
    width = w_ref.shape[1]
    half = w_ref.shape[0] // 2

    def part(d):
        at = pl.ds(pl.multiple_of(d * width, 16), width)
        return out_ref.at[pl.ds(half * c, half), at, :]

    def remote(src, dst, sent, got, peer):
        return pltpu.make_async_remote_copy(
            src, dst, send_sem.at[sent], recv_sem.at[got], device_id=peer, device_id_type=MESH
        )

    greet(xs + across, greet_line())
    own = w_ref.at[pl.ds(half * c, half)]
    mine = part(x * 2 + yh)
    theirs = part(x * 2 + 1 - yh)
    end = (yl == 0) | (yl == 3)
    base = 2 - 2 * (yl // 3)
    over = [
        remote(own, mine, n, 0, device(x, 1 - yh, z, base + n, c)) for n in range(2)
    ]

    @pl.when(end)
    def _():
        for copy in over:
            copy.start()

    sends = [remote(own, mine, 2 + n, 1 + n, peer) for n, peer in enumerate(xs)]
    for copy in sends:
        copy.start()
    exchange = Exchange(mix_ref, got_ref, own_sem, line_send, line_recv)
    exchange.start()
    local = pltpu.make_async_copy(own, mine, local_sem)
    local.start()
    over[0].wait_recv()
    for n, peer in enumerate(xs):
        copy = remote(theirs, theirs, 5 + n, 4 + n, peer)
        copy.start()
        sends.append(copy)
    local.wait()
    for copy in sends:
        copy.wait_recv()
    whole = out_ref.at[pl.ds(half * c, half)]
    copy = remote(whole, whole, 8, 7, pair)
    copy.start()
    exchange.wait()
    copy.wait_recv()
    for copy in sends + [copy]:
        copy.wait_send()

    @pl.when(end)
    def _():
        for copy in over:
            copy.wait_send()


def line_semaphores(n):
    return [
        pltpu.SemaphoreType.DMA,
        pltpu.SemaphoreType.DMA((n - 1,)),
        pltpu.SemaphoreType.DMA((n - 1,)),
    ]


def gather_weights(w, mix):
    n, width, d = w.shape
    vmem = pl.BlockSpec(memory_space=pltpu.VMEM)
    return pl.pallas_call(
        gather_kernel,
        out_shape=(
            jax.ShapeDtypeStruct((n, 8 * width, d), w.dtype),
            jax.ShapeDtypeStruct(mix.shape, mix.dtype),
        ),
        in_specs=[vmem] * 2,
        out_specs=(vmem,) * 2,
        scratch_shapes=[
            pltpu.SemaphoreType.DMA,
            pltpu.SemaphoreType.DMA((9,)),
            pltpu.SemaphoreType.DMA((8,)),
        ]
        + line_semaphores(mix.shape[0]),
        compiler_params=pltpu.CompilerParams(collective_id=1, has_side_effects=True),
        name="gather_weights",
    )(w, mix)


PIECES = (
    ((0, 0, 0, 48),),
    ((0, 48, 0, 32), (1, 0, 32, 16)),
    ((1, 16, 0, 48),),
    ((2, 0, 0, 48),),
    ((2, 48, 0, 32), (3, 0, 32, 16)),
    ((3, 16, 0, 48),),
)


class Sender:
    def __init__(self, send_sem, recv_sem):
        self.sems = (send_sem, recv_sem)
        self.started = []

    def __call__(self, src, dst, peer):
        n = len(self.started)
        copy = pltpu.make_async_remote_copy(
            src, dst, self.sems[0].at[n], self.sems[1].at[n],
            device_id=peer, device_id_type=MESH,
        )
        copy.start()
        self.started.append(copy)
        return copy

    def finish(self):
        for copy in self.started:
            copy.wait_send()


def landed(copies):
    for copy in copies:
        copy.wait_recv()


def back_kernel(
    mix_ref, gate_ref, up_ref, down_ref,
    got_ref, out_ref,
    wgot, xsend, xgot,
    send_sem, recv_sem, own_sem, line_send, line_recv,
):
    x, yh, z, yl, c = place()
    f32, bf16 = jnp.float32, jnp.bfloat16
    pair = device(x, yh, z, yl, 1 - c)
    xs = [device((x + k) % 4, yh, z, yl, c) for k in (1, 2, 3)]
    greet(xs, greet_line())
    send = Sender(send_sem, recv_sem)

    grads = (gate_ref, up_ref, down_ref)
    copies = [
        send(ref.at[pl.ds(2 * (1 - c), 2)], wgot.at[kind], pair)
        for kind, ref in enumerate(grads)
    ]
    exchange = Exchange(mix_ref, got_ref, own_sem, line_send, line_recv)
    exchange.start()
    for dest in range(4):
        for h in range(2):
            for q in range(4):
                xsend[dest, h * 4 + q, :, 96:128] = jnp.zeros((REP, 32), bf16)
            for q in (1, 3):
                xsend[dest, h * 4 + q, 64:REP] = jnp.zeros((REP - 64, 128), bf16)
    landed(copies)
    for dest in range(4):
        for h in range(2):
            first = (dest * 2 + h) * 48
            for i, pieces in enumerate(PIECES):
                kind, k = divmod(i, 2)
                for q, row, start, rows in pieces:
                    at = slice(first + start, first + start + rows)
                    total = grads[kind][2 * c + k, at, :].astype(f32)
                    total = total + wgot[kind, k, at, :].astype(f32)
                    xsend[dest, h * 4 + q, row : row + rows, 0:96] = total.astype(bf16)

    copies = [
        send(xsend.at[(x + k) % 4], xgot.at[k - 1], peer) for k, peer in zip((1, 2, 3), xs)
    ]
    exchange.wait()
    landed(copies)

    def add_x(n, carry):
        total = xsend[x, n].astype(f32)
        for k in range(3):
            total = total + xgot[k, n].astype(f32)
        out_ref[n] = total.astype(bf16)
        return carry

    lax.fori_loop(0, 8, add_x, 0)
    send.finish()


def exchange_back(mix, gate, up, down):
    vmem = pl.BlockSpec(memory_space=pltpu.VMEM)
    bf16 = jnp.bfloat16
    return pl.pallas_call(
        back_kernel,
        out_shape=(
            jax.ShapeDtypeStruct(mix.shape, mix.dtype),
            jax.ShapeDtypeStruct((8, REP, 128), bf16),
        ),
        in_specs=[vmem] * 4,
        out_specs=(vmem,) * 2,
        scratch_shapes=[
            pltpu.VMEM((3, 2, 384, 96), bf16),
            pltpu.VMEM((4, 8, REP, 128), bf16),
            pltpu.VMEM((3, 8, REP, 128), bf16),
            pltpu.SemaphoreType.DMA((6,)),
            pltpu.SemaphoreType.DMA((6,)),
        ]
        + line_semaphores(mix.shape[0]),
        compiler_params=pltpu.CompilerParams(collective_id=3, has_side_effects=True),
        name="exchange_back",
    )(mix, gate, up, down)


def sum_kernel(
    factor,
    part_ref, left_ref, right_ref, in_ref, outg_ref, norm_ref,
    out_ref,
    rep_ref, rgot, ysend, ygot, zall, yall, wother, repall,
    send_sem, recv_sem,
):
    x, yh, z, yl, c = place()
    f32, bf16 = jnp.float32, jnp.bfloat16
    y = yh * 4 + yl
    pair = device(x, yh, z, yl, 1 - c)
    xs = [device((x + k) % 4, yh, z, yl, c) for k in (1, 2, 3)]
    xo = [device((x + k) % 4, yh, z, yl, 1 - c) for k in (1, 2, 3)]
    near = [device(x, yh, z, (yl + k) % 4, c) for k in (1, 2, 3)]
    far = [device(x, 1 - yh, z, (yl + k) % 4, c) for k in (0, 1, 2, 3)]
    zs = [device(x, yh, (z + k) % 8, yl, c) for k in range(1, 8)]
    for k in range(4):
        for n in range(8):
            row, lane = (k % 2) * 128 + n * 16, (k // 2) * 128
            rep_ref[0, k, n] = left_ref[row : row + 16, lane : lane + 128].astype(bf16)
            rep_ref[1, k, n] = jnp.zeros((16, 128), bf16)
    for n in range(2):
        for j in range(2):
            at = slice(32 * j + 16 * n, 32 * j + 16 * n + 16)
            rep_ref[1, 0, n, :, 64 * j : 64 * j + 64] = right_ref[at, :].astype(bf16)
    gains = [
        ref[128 * t : 128 * t + 128].reshape(1, 128)
        for ref in (in_ref, outg_ref, norm_ref)
        for t in range(3)
    ]
    gains.append(jnp.zeros((7, 128), f32))
    rep_ref[1, 0, 2] = jnp.concatenate(gains, axis=0).astype(bf16)
    greet([pair] + xs + xo + near + far + zs)
    send = Sender(send_sem, recv_sem)

    copies = [send(rep_ref.at[1 - c, x], rgot.at[0], pair)]
    for k in (1, 2, 3):
        copies.append(send(rep_ref.at[c, (x + k) % 4], rgot.at[k], xs[k - 1]))
        copies.append(send(rep_ref.at[1 - c, (x + k) % 4], rgot.at[3 + k], xo[k - 1]))
    for n in range(8):
        ysend[n, 0:REP] = part_ref[n]
    landed(copies)
    total = rep_ref[c, x].astype(f32)
    for k in range(7):
        total = total + rgot[k].astype(f32)
    ysend[:, REP:SLOT, :] = total.astype(bf16)

    copies = [
        send(ysend.at[yh * 4 + (yl + k) % 4], ygot.at[k - 1], peer)
        for k, peer in zip((1, 2, 3), near)
    ]
    copies += [
        send(ysend.at[(1 - yh) * 4 + (yl + k) % 4], ygot.at[3 + k], peer)
        for k, peer in zip((0, 1, 2, 3), far)
    ]
    landed(copies)
    total = ysend[y].astype(f32)
    for k in range(7):
        total = total + ygot[k].astype(f32)
    zall[z] = total.astype(bf16)

    landed([send(zall.at[z], zall.at[z], peer) for peer in zs])
    total = zall[0].astype(f32)
    for k in range(1, 8):
        total = total + zall[k].astype(f32)
    yall[y] = total.astype(bf16)

    copies = [send(yall.at[y], yall.at[y], peer) for peer in near]
    tail = yall.at[y, REP:SLOT]
    copies += [send(tail, tail, peer) for peer in far]
    landed(copies)
    copies = [send(yall.at[pl.ds(4 * yh, 4)], wother, pair)]
    tails = yall.at[:, REP:SLOT]
    copies += [send(tails, repall.at[c, x], peer) for peer in [pair] + xs + xo]
    repall[c, x] = yall[:, REP:SLOT, :]

    def unpack(chunk, core):
        for i, pieces in enumerate(PIECES):
            kind, k = divmod(i, 2)
            for q, row, start, rows in pieces:
                at = pl.multiple_of(kind * 192 + (2 * core + k) * 48 + start, 16)
                value = chunk(q)[row : row + rows, 0:96].astype(f32) * factor
                out_ref[pl.ds(at, rows), 256:352] = value

    unpack(lambda q: yall.at[4 * yh + q], c)
    landed(copies)
    unpack(lambda q: wother.at[q], 1 - c)
    for k in range(4):
        for n in range(8):
            row, lane = (k % 2) * 128 + n * 16, (k // 2) * 128
            value = repall[0, k, n].astype(f32) * factor
            out_ref[row : row + 16, lane : lane + 128] = value
    for n in range(2):
        value = repall[1, 0, n].astype(f32) * factor
        out_ref[256 + n * 16 : 272 + n * 16, 0:64] = value[:, 0:64]
        out_ref[288 + n * 16 : 304 + n * 16, 0:64] = value[:, 64:128]
    value = repall[1, 0, 2].astype(f32) * factor
    for j in range(3):
        for t in range(3):
            row = value[3 * j + t : 3 * j + t + 1, :]
            out_ref[576 + j : 577 + j, t * 128 : t * 128 + 128] = row
    send.finish()


def sum_gradients(grads, factor):
    vmem = pl.BlockSpec(memory_space=pltpu.VMEM)
    bf16 = jnp.bfloat16
    copies = 7 + 7 + 7 + 7 + 8
    return pl.pallas_call(
        functools.partial(sum_kernel, factor),
        out_shape=jax.ShapeDtypeStruct((584, 384), jnp.float32),
        in_specs=[vmem] * len(grads),
        out_specs=vmem,
        scratch_shapes=[
            pltpu.VMEM((2, 4, 8, 16, 128), bf16),
            pltpu.VMEM((7, 8, 16, 128), bf16),
            pltpu.VMEM((8, SLOT, 128), bf16),
            pltpu.VMEM((7, SLOT, 128), bf16),
            pltpu.VMEM((8, SLOT, 128), bf16),
            pltpu.VMEM((8, SLOT, 128), bf16),
            pltpu.VMEM((4, SLOT, 128), bf16),
            pltpu.VMEM((2, 4, 8, 16, 128), bf16),
            pltpu.SemaphoreType.DMA((copies,)),
            pltpu.SemaphoreType.DMA((copies,)),
        ],
        compiler_params=pltpu.CompilerParams(collective_id=2, has_side_effects=True),
        name="sum_gradients",
    )(*grads)


def shards(
    points,
    cotangent,
    in_gain,
    out_gain,
    left_factor,
    right_factor,
    norm_gain,
    gate_weight,
    up_weight,
    down_weight,
):
    seq_count = lax.axis_size("seq")
    data_count = lax.axis_size("dp")
    row_count = points.shape[1]
    channels = points.shape[2]
    block_size = left_factor.shape[0]
    block_total = right_factor.shape[0]
    blocks = row_count // block_size
    shard_width = gate_weight.shape[2]
    nblocks, block_in = gate_weight.shape[:2]
    block_hidden = data_count * shard_width
    quarter = block_hidden // nblocks
    packed = jnp.concatenate([gate_weight, up_weight, down_weight], axis=0).transpose(0, 2, 1)
    inputs = points[0].astype(jnp.float32)
    scaled = (inputs * in_gain).astype(jnp.bfloat16).reshape(blocks, block_size, channels)
    first_mix = jnp.einsum(
        "pb,abc->apc", left_factor, scaled, preferred_element_type=jnp.float32
    ).astype(jnp.bfloat16)
    weights, received = gather_weights(
        packed, first_mix.reshape(seq_count, block_size // seq_count, channels)
    )
    gate_full, up_full, down_full = weights[0:4], weights[4:8], weights[8:12]
    down_grid = down_full.reshape(nblocks, nblocks, quarter, block_in)
    mixed = jnp.einsum("qa,apc->pqc", right_factor, received, preferred_element_type=jnp.float32)
    first_moved = received
    mixed = mixed.reshape(row_count, channels)
    residual = inputs + out_gain * mixed
    inv_rms = lax.rsqrt(jnp.mean(residual * residual, axis=-1, keepdims=True) + 1e-05)
    normed = residual * inv_rms
    hidden_in = (normed * norm_gain).astype(jnp.bfloat16).reshape(row_count, nblocks, block_in)
    gate_pre = jnp.einsum("rkd,kfd->rkf", hidden_in, gate_full, preferred_element_type=jnp.float32)
    up_pre = jnp.einsum("rkd,kfd->rkf", hidden_in, up_full, preferred_element_type=jnp.float32)
    sig_gate = jax.nn.sigmoid(gate_pre)
    act_gate = gate_pre * sig_gate
    hidden = (act_gate * up_pre).astype(jnp.bfloat16)
    hidden_grid = hidden.reshape(row_count, nblocks, nblocks, quarter)
    branch = jnp.einsum(
        "rkjf,jkfo->rjo", hidden_grid, down_grid, preferred_element_type=jnp.float32
    ).reshape(row_count, channels)
    layer_out = (residual + branch).astype(jnp.bfloat16)
    grad_grid = cotangent[0].reshape(row_count, nblocks, block_in)
    dhidden = jnp.einsum(
        "rjo,jkfo->rkjf", grad_grid, down_grid, preferred_element_type=jnp.float32
    ).reshape(row_count, nblocks, block_hidden)
    grad_down = jnp.einsum(
        "rjo,rkjf->jkfo", grad_grid, hidden_grid, preferred_element_type=jnp.float32
    ).reshape(nblocks, block_hidden, block_in)
    dgate = (dhidden * up_pre * sig_gate * (1.0 + gate_pre * (1.0 - sig_gate))).astype(jnp.bfloat16)
    dupper = (dhidden * act_gate).astype(jnp.bfloat16)
    dhid_in = jnp.einsum("rkf,kfd->rkd", dgate, gate_full, preferred_element_type=jnp.float32)
    dhid_in = (
        dhid_in + jnp.einsum("rkf,kfd->rkd", dupper, up_full, preferred_element_type=jnp.float32)
    ).reshape(row_count, channels)
    grad_gate = jnp.einsum("rkd,rkf->kfd", hidden_in, dgate, preferred_element_type=jnp.float32)
    grad_up = jnp.einsum("rkd,rkf->kfd", hidden_in, dupper, preferred_element_type=jnp.float32)
    grad_norm = jnp.sum(dhid_in * normed, axis=0)
    scaled_grad = dhid_in * norm_gain
    dresid = cotangent[0].astype(jnp.float32) + inv_rms * (
        scaled_grad - normed * jnp.mean(scaled_grad * normed, axis=-1, keepdims=True)
    )
    grad_out = jnp.sum(dresid * mixed, axis=0)
    dmixed = (
        (dresid * out_gain)
        .astype(jnp.bfloat16)
        .reshape(block_size // seq_count, block_total, channels)
    )
    dfirst = jnp.einsum(
        "qa,pqc->apc", right_factor, dmixed, preferred_element_type=jnp.float32
    ).astype(jnp.bfloat16)
    grad_right = jnp.einsum("pqc,apc->qa", dmixed, first_moved, preferred_element_type=jnp.float32)
    received, partial = exchange_back(
        dfirst,
        grad_gate.astype(jnp.bfloat16),
        grad_up.astype(jnp.bfloat16),
        grad_down.astype(jnp.bfloat16),
    )
    received = received.reshape(1, block_size, channels)
    dscaled = jnp.einsum("pb,apc->abc", left_factor, received, preferred_element_type=jnp.float32)
    grad_left = jnp.einsum("apc,abc->pb", received, scaled, preferred_element_type=jnp.float32)
    dscaled = dscaled.reshape(row_count, channels)
    grad_in = jnp.sum(dscaled * inputs, axis=0)
    grad_points = (dresid + dscaled * in_gain).astype(jnp.bfloat16)
    factor = float(data_count * row_count * seq_count) ** (-0.5)
    sums = sum_gradients(
        (
            partial,
            grad_left,
            grad_right,
            grad_in,
            grad_out,
            grad_norm,
        ),
        factor,
    )

    def weight(n):
        part = sums[192 * n : 192 * n + 192, 256:352]
        return part.reshape(nblocks, shard_width, block_in).transpose(0, 2, 1)

    return (
        layer_out[None],
        grad_points[None],
        sums[0:256, 0:256],
        sums[256:320, 0:64],
        sums[576],
        sums[577],
        sums[578],
        weight(0),
        weight(1),
        weight(2),
    )


def solution(mesh):
    in_specs = (
        P("dp", "seq", None),
        P("dp", "seq", None),
        P(),
        P(),
        P(),
        P(),
        P(),
        P(None, None, "dp"),
        P(None, None, "dp"),
        P(None, None, "dp"),
    )
    out_specs = (
        P("dp", "seq", None),
        P("dp", "seq", None),
        P(),
        P(),
        P(),
        P(),
        P(),
        P(None, None, "dp"),
        P(None, None, "dp"),
        P(None, None, "dp"),
    )
    return jax.shard_map(shards, mesh=mesh, in_specs=in_specs, out_specs=out_specs, check_vma=False)
```

```python
import functools

import jax
import jax.numpy as jnp
from jax import lax
from jax.experimental import pallas as pl
from jax.experimental.pallas import tpu as pltpu
from jax.sharding import PartitionSpec as P

MESH = pl.DeviceIdType.MESH
ROWS = 80


def place():
    d = lax.axis_index("dp")
    s = lax.axis_index("seq")
    return d // 2, d % 2, s // 8, (s // 2) % 4, s % 2


def device(x, yh, z, yl, c):
    return (x * 2 + yh, (z * 4 + yl) * 2 + c)


def greet(peers, others=0):
    barrier = pltpu.get_barrier_semaphore()
    for peer in peers:
        pl.semaphore_signal(barrier, inc=1, device_id=peer, device_id_type=MESH)
    pl.semaphore_wait(barrier, len(peers) + others)


def line():
    d, s, n = lax.axis_index("dp"), lax.axis_index("seq"), lax.axis_size("seq")
    return d, s, n


def greet_line():
    d, s, n = line()
    barrier = pltpu.get_barrier_semaphore()

    def signal(k, carry):
        pl.semaphore_signal(
            barrier, inc=1, device_id=(d, (s + k) % n), device_id_type=MESH
        )
        return carry

    lax.fori_loop(1, n, signal, 0)
    return n - 1


class Exchange:
    def __init__(self, src, dst, local_sem, send_sem, recv_sem):
        self.refs = (src, dst)
        self.sems = (send_sem, recv_sem)
        s = lax.axis_index("seq")
        self.local = pltpu.make_async_copy(src.at[s], dst.at[s], local_sem)

    def copy(self, k):
        d, s, n = line()
        peer = (s + k) % n
        return pltpu.make_async_remote_copy(
            self.refs[0].at[peer], self.refs[1].at[s],
            self.sems[0].at[k - 1], self.sems[1].at[k - 1],
            device_id=(d, peer), device_id_type=MESH,
        )

    def start(self):
        def one(k, carry):
            self.copy(k).start()
            return carry

        lax.fori_loop(1, line()[2], one, 0)
        self.local.start()

    def wait(self):
        def one(k, carry):
            self.copy(k).wait()
            return carry

        self.local.wait()
        lax.fori_loop(1, line()[2], one, 0)


def gather_kernel(
    w_ref, mix_ref, out_ref, got_ref,
    local_sem, send_sem, recv_sem, own_sem, line_send, line_recv,
):
    x, yh, z, yl, c = place()
    pair = device(x, yh, z, yl, 1 - c)
    xs = [device((x + k) % 4, yh, z, yl, c) for k in (1, 2, 3)]
    across = [device(x, 1 - yh, z, k, c) for k in range(4)]
    width = w_ref.shape[1]
    half = w_ref.shape[0] // 2

    def part(d):
        at = pl.ds(pl.multiple_of(d * width, 16), width)
        return out_ref.at[pl.ds(half * c, half), at, :]

    def remote(src, dst, sent, got, peer):
        return pltpu.make_async_remote_copy(
            src, dst, send_sem.at[sent], recv_sem.at[got], device_id=peer, device_id_type=MESH
        )

    greet(xs + across, greet_line())
    own = w_ref.at[pl.ds(half * c, half)]
    mine = part(x * 2 + yh)
    theirs = part(x * 2 + 1 - yh)
    end = (yl == 0) | (yl == 3)
    base = 2 - 2 * (yl // 3)
    over = [
        remote(own, mine, n, 0, device(x, 1 - yh, z, base + n, c)) for n in range(2)
    ]

    @pl.when(end)
    def _():
        for copy in over:
            copy.start()

    sends = [remote(own, mine, 2 + n, 1 + n, peer) for n, peer in enumerate(xs)]
    for copy in sends:
        copy.start()
    exchange = Exchange(mix_ref, got_ref, own_sem, line_send, line_recv)
    exchange.start()
    local = pltpu.make_async_copy(own, mine, local_sem)
    local.start()
    over[0].wait_recv()
    for n, peer in enumerate(xs):
        copy = remote(theirs, theirs, 5 + n, 4 + n, peer)
        copy.start()
        sends.append(copy)
    local.wait()
    for copy in sends:
        copy.wait_recv()
    whole = out_ref.at[pl.ds(half * c, half)]
    copy = remote(whole, whole, 8, 7, pair)
    copy.start()
    exchange.wait()
    copy.wait_recv()
    for copy in sends + [copy]:
        copy.wait_send()

    @pl.when(end)
    def _():
        for copy in over:
            copy.wait_send()


def line_semaphores(n):
    return [
        pltpu.SemaphoreType.DMA,
        pltpu.SemaphoreType.DMA((n - 1,)),
        pltpu.SemaphoreType.DMA((n - 1,)),
    ]


def gather_weights(w, mix):
    n, width, d = w.shape
    vmem = pl.BlockSpec(memory_space=pltpu.VMEM)
    return pl.pallas_call(
        gather_kernel,
        out_shape=(
            jax.ShapeDtypeStruct((n, 8 * width, d), w.dtype),
            jax.ShapeDtypeStruct(mix.shape, mix.dtype),
        ),
        in_specs=[vmem] * 2,
        out_specs=(vmem,) * 2,
        scratch_shapes=[
            pltpu.SemaphoreType.DMA,
            pltpu.SemaphoreType.DMA((9,)),
            pltpu.SemaphoreType.DMA((8,)),
        ]
        + line_semaphores(mix.shape[0]),
        compiler_params=pltpu.CompilerParams(collective_id=1, has_side_effects=True),
        name="gather_weights",
    )(w, mix)


PIECES = (
    ((0, 0, 0, 48),),
    ((0, 48, 0, 32), (1, 0, 32, 16)),
    ((1, 16, 0, 48),),
    ((2, 0, 0, 48),),
    ((2, 48, 0, 32), (3, 0, 32, 16)),
    ((3, 16, 0, 48),),
)


class Sender:
    def __init__(self, send_sem, recv_sem):
        self.sems = (send_sem, recv_sem)
        self.started = []

    def __call__(self, src, dst, peer):
        n = len(self.started)
        copy = pltpu.make_async_remote_copy(
            src, dst, self.sems[0].at[n], self.sems[1].at[n],
            device_id=peer, device_id_type=MESH,
        )
        copy.start()
        self.started.append(copy)
        return copy

    def finish(self):
        for copy in self.started:
            copy.wait_send()


def landed(copies):
    for copy in copies:
        copy.wait_recv()


def back_kernel(
    mix_ref, gate_ref, up_ref, down_ref,
    got_ref, out_ref,
    wgot, xsend, xgot,
    send_sem, recv_sem, own_sem, line_send, line_recv,
):
    x, yh, z, yl, c = place()
    f32, bf16 = jnp.float32, jnp.bfloat16
    pair = device(x, yh, z, yl, 1 - c)
    xs = [device((x + k) % 4, yh, z, yl, c) for k in (1, 2, 3)]
    greet(xs, greet_line())
    send = Sender(send_sem, recv_sem)

    grads = (gate_ref, up_ref, down_ref)
    copies = [
        send(ref.at[pl.ds(2 * (1 - c), 2)], wgot.at[kind], pair)
        for kind, ref in enumerate(grads)
    ]
    exchange = Exchange(mix_ref, got_ref, own_sem, line_send, line_recv)
    exchange.start()
    for dest in range(4):
        for h in range(2):
            for q in range(4):
                xsend[dest, h * 4 + q, :, 96:128] = jnp.zeros((ROWS, 32), bf16)
            for q in (1, 3):
                xsend[dest, h * 4 + q, 64:ROWS] = jnp.zeros((ROWS - 64, 128), bf16)
    landed(copies)
    for dest in range(4):
        for h in range(2):
            first = (dest * 2 + h) * 48
            for i, pieces in enumerate(PIECES):
                kind, k = divmod(i, 2)
                for q, row, start, rows in pieces:
                    at = slice(first + start, first + start + rows)
                    total = grads[kind][2 * c + k, at, :].astype(f32)
                    total = total + wgot[kind, k, at, :].astype(f32)
                    xsend[dest, h * 4 + q, row : row + rows, 0:96] = total.astype(bf16)

    copies = [
        send(xsend.at[(x + k) % 4], xgot.at[k - 1], peer) for k, peer in zip((1, 2, 3), xs)
    ]
    exchange.wait()
    landed(copies)

    def add_x(n, carry):
        total = xsend[x, n].astype(f32)
        for k in range(3):
            total = total + xgot[k, n].astype(f32)
        out_ref[n] = total.astype(bf16)
        return carry

    lax.fori_loop(0, 8, add_x, 0)
    send.finish()


def exchange_back(mix, gate, up, down):
    vmem = pl.BlockSpec(memory_space=pltpu.VMEM)
    bf16 = jnp.bfloat16
    return pl.pallas_call(
        back_kernel,
        out_shape=(
            jax.ShapeDtypeStruct(mix.shape, mix.dtype),
            jax.ShapeDtypeStruct((8, ROWS, 128), bf16),
        ),
        in_specs=[vmem] * 4,
        out_specs=(vmem,) * 2,
        scratch_shapes=[
            pltpu.VMEM((3, 2, 384, 96), bf16),
            pltpu.VMEM((4, 8, ROWS, 128), bf16),
            pltpu.VMEM((3, 8, ROWS, 128), bf16),
            pltpu.SemaphoreType.DMA((6,)),
            pltpu.SemaphoreType.DMA((6,)),
        ]
        + line_semaphores(mix.shape[0]),
        compiler_params=pltpu.CompilerParams(collective_id=3, has_side_effects=True),
        name="exchange_back",
    )(mix, gate, up, down)


def sum_kernel(
    factor,
    part_ref, left_ref, right_ref, in_ref, outg_ref, norm_ref,
    out_ref,
    rep_ref, rgot, ysend, ygot, zall, yall, repall, wgot, wzall, wyall, wother,
    send_sem, recv_sem,
):
    x, yh, z, yl, c = place()
    f32, bf16 = jnp.float32, jnp.bfloat16
    y = yh * 4 + yl
    pair = device(x, yh, z, yl, 1 - c)
    xs = [device((x + k) % 4, yh, z, yl, c) for k in (1, 2, 3)]
    xo = [device((x + k) % 4, yh, z, yl, 1 - c) for k in (1, 2, 3)]
    near = [device(x, yh, z, (yl + k) % 4, c) for k in (1, 2, 3)]
    far = [device(x, 1 - yh, z, (yl + k) % 4, c) for k in (0, 1, 2, 3)]
    zs = [device(x, yh, (z + k) % 8, yl, c) for k in range(1, 8)]
    for k in range(4):
        for n in range(8):
            row, lane = (k % 2) * 128 + n * 16, (k // 2) * 128
            rep_ref[0, k, n] = left_ref[row : row + 16, lane : lane + 128].astype(bf16)
            rep_ref[1, k, n] = jnp.zeros((16, 128), bf16)
    for n in range(2):
        for j in range(2):
            at = slice(32 * j + 16 * n, 32 * j + 16 * n + 16)
            rep_ref[1, 0, n, :, 64 * j : 64 * j + 64] = right_ref[at, :].astype(bf16)
    gains = [
        ref[128 * t : 128 * t + 128].reshape(1, 128)
        for ref in (in_ref, outg_ref, norm_ref)
        for t in range(3)
    ]
    gains.append(jnp.zeros((7, 128), f32))
    rep_ref[1, 0, 2] = jnp.concatenate(gains, axis=0).astype(bf16)
    greet([pair] + xs + xo + near + far + zs)
    send = Sender(send_sem, recv_sem)

    copies = [send(rep_ref.at[1 - c, x], rgot.at[0], pair)]
    for k in (1, 2, 3):
        copies.append(send(rep_ref.at[c, (x + k) % 4], rgot.at[k], xs[k - 1]))
        copies.append(send(rep_ref.at[1 - c, (x + k) % 4], rgot.at[3 + k], xo[k - 1]))

    def along_y(src, dst):
        sent = [
            send(src.at[yh * 4 + (yl + k) % 4], dst.at[k - 1], peer)
            for k, peer in zip((1, 2, 3), near)
        ]
        return sent + [
            send(src.at[(1 - yh) * 4 + (yl + k) % 4], dst.at[3 + k], peer)
            for k, peer in zip((0, 1, 2, 3), far)
        ]

    def add(first, others):
        total = first.astype(f32)
        for k in range(others.shape[0]):
            total = total + others[k].astype(f32)
        return total.astype(bf16)

    def add_all(parts):
        total = parts[0].astype(f32)
        for k in range(1, 8):
            total = total + parts[k].astype(f32)
        return total.astype(bf16)

    w_y = along_y(part_ref, wgot)
    landed(copies)
    ysend[...] = add(rep_ref[c, x], rgot)
    r_y = along_y(ysend, ygot)
    landed(w_y)
    wzall[z] = add(part_ref[y], wgot)
    w_z = [send(wzall.at[z], wzall.at[z], peer) for peer in zs]
    landed(r_y)
    zall[z] = add(ysend[y], ygot)
    r_z = [send(zall.at[z], zall.at[z], peer) for peer in zs]
    landed(r_z)
    yall[y] = add_all(zall)
    r_back = [send(yall.at[y], yall.at[y], peer) for peer in near + far]
    landed(w_z)
    wyall[yl] = add_all(wzall)
    w_back = [send(wyall.at[yl], wyall.at[yl], peer) for peer in near]
    landed(r_back)
    copies = [send(yall, repall.at[c, x], peer) for peer in [pair] + xs + xo]
    repall[c, x] = yall[...]
    landed(w_back)
    w_pair = send(wyall, wother, pair)

    def unpack(chunk, core):
        for i, pieces in enumerate(PIECES):
            kind, k = divmod(i, 2)
            for q, row, start, rows in pieces:
                at = pl.multiple_of(kind * 192 + (2 * core + k) * 48 + start, 16)
                value = chunk[q, row : row + rows, 0:96].astype(f32) * factor
                out_ref[pl.ds(at, rows), 256:352] = value

    unpack(wyall, c)
    landed([w_pair])
    unpack(wother, 1 - c)
    landed(copies)
    for k in range(4):
        for n in range(8):
            row, lane = (k % 2) * 128 + n * 16, (k // 2) * 128
            value = repall[0, k, n].astype(f32) * factor
            out_ref[row : row + 16, lane : lane + 128] = value
    for n in range(2):
        value = repall[1, 0, n].astype(f32) * factor
        out_ref[256 + n * 16 : 272 + n * 16, 0:64] = value[:, 0:64]
        out_ref[288 + n * 16 : 304 + n * 16, 0:64] = value[:, 64:128]
    value = repall[1, 0, 2].astype(f32) * factor
    for j in range(3):
        for t in range(3):
            row = value[3 * j + t : 3 * j + t + 1, :]
            out_ref[576 + j : 577 + j, t * 128 : t * 128 + 128] = row
    send.finish()


def sum_gradients(grads, factor):
    vmem = pl.BlockSpec(memory_space=pltpu.VMEM)
    bf16 = jnp.bfloat16
    copies = 7 * 7 + 3 + 1
    return pl.pallas_call(
        functools.partial(sum_kernel, factor),
        out_shape=jax.ShapeDtypeStruct((584, 384), jnp.float32),
        in_specs=[vmem] * len(grads),
        out_specs=vmem,
        scratch_shapes=[
            pltpu.VMEM((2, 4, 8, 16, 128), bf16),
            pltpu.VMEM((7, 8, 16, 128), bf16),
            pltpu.VMEM((8, 16, 128), bf16),
            pltpu.VMEM((7, 16, 128), bf16),
            pltpu.VMEM((8, 16, 128), bf16),
            pltpu.VMEM((8, 16, 128), bf16),
            pltpu.VMEM((2, 4, 8, 16, 128), bf16),
            pltpu.VMEM((7, ROWS, 128), bf16),
            pltpu.VMEM((8, ROWS, 128), bf16),
            pltpu.VMEM((4, ROWS, 128), bf16),
            pltpu.VMEM((4, ROWS, 128), bf16),
            pltpu.SemaphoreType.DMA((copies,)),
            pltpu.SemaphoreType.DMA((copies,)),
        ],
        compiler_params=pltpu.CompilerParams(collective_id=2, has_side_effects=True),
        name="sum_gradients",
    )(*grads)


def split_kernel(sums_ref, left, right, gain_in, gain_out, norm, gate, up, down):
    left[...] = sums_ref[0:256, 0:256]
    right[...] = sums_ref[256:320, 0:64]
    for j, ref in enumerate((gain_in, gain_out, norm)):
        for t in range(3):
            row = sums_ref[576 + j : 577 + j, 128 * t : 128 * t + 128]
            ref[128 * t : 128 * t + 128] = row.reshape(128)
    for j, ref in enumerate((gate, up, down)):
        for k in range(4):
            at = 192 * j + 48 * k
            ref[k] = sums_ref[at : at + 48, 256:352]


def split_sums(sums):
    vmem = pl.BlockSpec(memory_space=pltpu.VMEM)
    shapes = [(256, 256), (64, 64)] + [(384,)] * 3 + [(4, 48, 96)] * 3
    return pl.pallas_call(
        split_kernel,
        out_shape=[jax.ShapeDtypeStruct(shape, jnp.float32) for shape in shapes],
        in_specs=[vmem],
        out_specs=[vmem] * len(shapes),
        name="split_sums",
    )(sums)


def shards(
    points,
    cotangent,
    in_gain,
    out_gain,
    left_factor,
    right_factor,
    norm_gain,
    gate_weight,
    up_weight,
    down_weight,
):
    seq_count = lax.axis_size("seq")
    data_count = lax.axis_size("dp")
    row_count = points.shape[1]
    channels = points.shape[2]
    block_size = left_factor.shape[0]
    block_total = right_factor.shape[0]
    blocks = row_count // block_size
    shard_width = gate_weight.shape[2]
    nblocks, block_in = gate_weight.shape[:2]
    block_hidden = data_count * shard_width
    quarter = block_hidden // nblocks
    packed = jnp.concatenate([gate_weight, up_weight, down_weight], axis=0).transpose(0, 2, 1)
    inputs = points[0].astype(jnp.float32)
    scaled = (inputs * in_gain).astype(jnp.bfloat16).reshape(blocks, block_size, channels)
    first_mix = jnp.einsum(
        "pb,abc->apc", left_factor, scaled, preferred_element_type=jnp.float32
    ).astype(jnp.bfloat16)
    weights, received = gather_weights(
        packed, first_mix.reshape(seq_count, block_size // seq_count, channels)
    )
    gate_full, up_full, down_full = weights[0:4], weights[4:8], weights[8:12]
    down_grid = down_full.reshape(nblocks, nblocks, quarter, block_in)
    mixed = jnp.einsum("qa,apc->pqc", right_factor, received, preferred_element_type=jnp.float32)
    first_moved = received
    mixed = mixed.reshape(row_count, channels)
    residual = inputs + out_gain * mixed
    inv_rms = lax.rsqrt(jnp.mean(residual * residual, axis=-1, keepdims=True) + 1e-05)
    normed = residual * inv_rms
    hidden_in = (normed * norm_gain).astype(jnp.bfloat16).reshape(row_count, nblocks, block_in)
    gate_pre = jnp.einsum("rkd,kfd->rkf", hidden_in, gate_full, preferred_element_type=jnp.float32)
    up_pre = jnp.einsum("rkd,kfd->rkf", hidden_in, up_full, preferred_element_type=jnp.float32)
    sig_gate = jax.nn.sigmoid(gate_pre)
    act_gate = gate_pre * sig_gate
    hidden = (act_gate * up_pre).astype(jnp.bfloat16)
    hidden_grid = hidden.reshape(row_count, nblocks, nblocks, quarter)
    branch = jnp.einsum(
        "rkjf,jkfo->rjo", hidden_grid, down_grid, preferred_element_type=jnp.float32
    ).reshape(row_count, channels)
    layer_out = (residual + branch).astype(jnp.bfloat16)
    grad_grid = cotangent[0].reshape(row_count, nblocks, block_in)
    dhidden = jnp.einsum(
        "rjo,jkfo->rkjf", grad_grid, down_grid, preferred_element_type=jnp.float32
    ).reshape(row_count, nblocks, block_hidden)
    grad_down = jnp.einsum(
        "rjo,rkjf->jkfo", grad_grid, hidden_grid, preferred_element_type=jnp.float32
    ).reshape(nblocks, block_hidden, block_in)
    dgate = (dhidden * up_pre * sig_gate * (1.0 + gate_pre * (1.0 - sig_gate))).astype(jnp.bfloat16)
    dupper = (dhidden * act_gate).astype(jnp.bfloat16)
    dhid_in = jnp.einsum("rkf,kfd->rkd", dgate, gate_full, preferred_element_type=jnp.float32)
    dhid_in = (
        dhid_in + jnp.einsum("rkf,kfd->rkd", dupper, up_full, preferred_element_type=jnp.float32)
    ).reshape(row_count, channels)
    grad_gate = jnp.einsum("rkd,rkf->kfd", hidden_in, dgate, preferred_element_type=jnp.float32)
    grad_up = jnp.einsum("rkd,rkf->kfd", hidden_in, dupper, preferred_element_type=jnp.float32)
    grad_norm = jnp.sum(dhid_in * normed, axis=0)
    scaled_grad = dhid_in * norm_gain
    dresid = cotangent[0].astype(jnp.float32) + inv_rms * (
        scaled_grad - normed * jnp.mean(scaled_grad * normed, axis=-1, keepdims=True)
    )
    grad_out = jnp.sum(dresid * mixed, axis=0)
    dmixed = (
        (dresid * out_gain)
        .astype(jnp.bfloat16)
        .reshape(block_size // seq_count, block_total, channels)
    )
    dfirst = jnp.einsum(
        "qa,pqc->apc", right_factor, dmixed, preferred_element_type=jnp.float32
    ).astype(jnp.bfloat16)
    grad_right = jnp.einsum("pqc,apc->qa", dmixed, first_moved, preferred_element_type=jnp.float32)
    received, partial = exchange_back(
        dfirst,
        grad_gate.astype(jnp.bfloat16),
        grad_up.astype(jnp.bfloat16),
        grad_down.astype(jnp.bfloat16),
    )
    received = received.reshape(1, block_size, channels)
    dscaled = jnp.einsum("pb,apc->abc", left_factor, received, preferred_element_type=jnp.float32)
    grad_left = jnp.einsum("apc,abc->pb", received, scaled, preferred_element_type=jnp.float32)
    dscaled = dscaled.reshape(row_count, channels)
    grad_in = jnp.sum(dscaled * inputs, axis=0)
    grad_points = (dresid + dscaled * in_gain).astype(jnp.bfloat16)
    factor = float(data_count * row_count * seq_count) ** (-0.5)
    sums = sum_gradients(
        (
            partial,
            grad_left,
            grad_right,
            grad_in,
            grad_out,
            grad_norm,
        ),
        factor,
    )

    left_sum, right_sum, in_sum, out_sum, norm_sum, *w_sums = split_sums(sums)
    return (
        layer_out[None],
        grad_points[None],
        left_sum,
        right_sum,
        in_sum,
        out_sum,
        norm_sum,
        *(w_sum.transpose(0, 2, 1) for w_sum in w_sums),
    )


def solution(mesh):
    in_specs = (
        P("dp", "seq", None),
        P("dp", "seq", None),
        P(),
        P(),
        P(),
        P(),
        P(),
        P(None, None, "dp"),
        P(None, None, "dp"),
        P(None, None, "dp"),
    )
    out_specs = (
        P("dp", "seq", None),
        P("dp", "seq", None),
        P(),
        P(),
        P(),
        P(),
        P(),
        P(None, None, "dp"),
        P(None, None, "dp"),
        P(None, None, "dp"),
    )
    return jax.shard_map(shards, mesh=mesh, in_specs=in_specs, out_specs=out_specs, check_vma=False)
```

```python
import functools

import jax
import jax.numpy as jnp
from jax import lax
from jax.experimental import pallas as pl
from jax.experimental.pallas import tpu as pltpu
from jax.sharding import PartitionSpec as P

MESH = pl.DeviceIdType.MESH
ROWS = 80


def place():
    d = lax.axis_index("dp")
    s = lax.axis_index("seq")
    return d // 2, d % 2, s // 8, (s // 2) % 4, s % 2


def device(x, yh, z, yl, c):
    return (x * 2 + yh, (z * 4 + yl) * 2 + c)


def signal(peers):
    barrier = pltpu.get_barrier_semaphore()
    for peer in peers:
        pl.semaphore_signal(barrier, inc=1, device_id=peer, device_id_type=MESH)


def await_all(count):
    pl.semaphore_wait(pltpu.get_barrier_semaphore(), count)


def greet(peers, others=0):
    signal(peers)
    await_all(len(peers) + others)


def line():
    d, s, n = lax.axis_index("dp"), lax.axis_index("seq"), lax.axis_size("seq")
    return d, s, n


def greet_line():
    d, s, n = line()
    barrier = pltpu.get_barrier_semaphore()

    def one(k, carry):
        pl.semaphore_signal(
            barrier, inc=1, device_id=(d, (s + k) % n), device_id_type=MESH
        )
        return carry

    lax.fori_loop(1, n, one, 0)
    return n - 1


class Exchange:
    def __init__(self, src, dst, local_sem, send_sem, recv_sem):
        self.refs = (src, dst)
        self.sems = (send_sem, recv_sem)
        s = lax.axis_index("seq")
        self.local = pltpu.make_async_copy(src.at[s], dst.at[s], local_sem)

    def copy(self, k):
        d, s, n = line()
        peer = (s + k) % n
        return pltpu.make_async_remote_copy(
            self.refs[0].at[peer], self.refs[1].at[s],
            self.sems[0].at[k - 1], self.sems[1].at[k - 1],
            device_id=(d, peer), device_id_type=MESH,
        )

    def start(self):
        def one(k, carry):
            self.copy(k).start()
            return carry

        lax.fori_loop(1, line()[2], one, 0)
        self.local.start()

    def wait(self):
        def one(k, carry):
            self.copy(k).wait()
            return carry

        self.local.wait()
        lax.fori_loop(1, line()[2], one, 0)


def gather_kernel(
    w_ref, mix_ref, out_ref, got_ref,
    local_sem, send_sem, recv_sem, own_sem, line_send, line_recv,
):
    x, yh, z, yl, c = place()
    pair = device(x, yh, z, yl, 1 - c)
    xs = [device((x + k) % 4, yh, z, yl, c) for k in (1, 2, 3)]
    across = [device(x, 1 - yh, z, k, c) for k in range(4)]
    width = w_ref.shape[1]
    half = w_ref.shape[0] // 2

    def part(d):
        at = pl.ds(pl.multiple_of(d * width, 16), width)
        return out_ref.at[pl.ds(half * c, half), at, :]

    def remote(src, dst, sent, got, peer):
        return pltpu.make_async_remote_copy(
            src, dst, send_sem.at[sent], recv_sem.at[got], device_id=peer, device_id_type=MESH
        )

    greet(xs + across, greet_line())
    own = w_ref.at[pl.ds(half * c, half)]
    mine = part(x * 2 + yh)
    theirs = part(x * 2 + 1 - yh)
    end = (yl == 0) | (yl == 3)
    base = 2 - 2 * (yl // 3)
    over = [
        remote(own, mine, n, 0, device(x, 1 - yh, z, base + n, c)) for n in range(2)
    ]

    @pl.when(end)
    def _():
        for copy in over:
            copy.start()

    sends = [remote(own, mine, 2 + n, 1 + n, peer) for n, peer in enumerate(xs)]
    for copy in sends:
        copy.start()
    exchange = Exchange(mix_ref, got_ref, own_sem, line_send, line_recv)
    exchange.start()
    local = pltpu.make_async_copy(own, mine, local_sem)
    local.start()
    over[0].wait_recv()
    for n, peer in enumerate(xs):
        copy = remote(theirs, theirs, 5 + n, 4 + n, peer)
        copy.start()
        sends.append(copy)
    local.wait()
    for copy in sends:
        copy.wait_recv()
    whole = out_ref.at[pl.ds(half * c, half)]
    copy = remote(whole, whole, 8, 7, pair)
    copy.start()
    exchange.wait()
    copy.wait_recv()
    for copy in sends + [copy]:
        copy.wait_send()

    @pl.when(end)
    def _():
        for copy in over:
            copy.wait_send()


def line_semaphores(n):
    return [
        pltpu.SemaphoreType.DMA,
        pltpu.SemaphoreType.DMA((n - 1,)),
        pltpu.SemaphoreType.DMA((n - 1,)),
    ]


def gather_weights(w, mix):
    n, width, d = w.shape
    vmem = pl.BlockSpec(memory_space=pltpu.VMEM)
    return pl.pallas_call(
        gather_kernel,
        out_shape=(
            jax.ShapeDtypeStruct((n, 8 * width, d), w.dtype),
            jax.ShapeDtypeStruct(mix.shape, mix.dtype),
        ),
        in_specs=[vmem] * 2,
        out_specs=(vmem,) * 2,
        scratch_shapes=[
            pltpu.SemaphoreType.DMA,
            pltpu.SemaphoreType.DMA((9,)),
            pltpu.SemaphoreType.DMA((8,)),
        ]
        + line_semaphores(mix.shape[0]),
        compiler_params=pltpu.CompilerParams(collective_id=1, has_side_effects=True),
        name="gather_weights",
    )(w, mix)


PIECES = (
    ((0, 0, 0, 48),),
    ((0, 48, 0, 32), (1, 0, 32, 16)),
    ((1, 16, 0, 48),),
    ((2, 0, 0, 48),),
    ((2, 48, 0, 32), (3, 0, 32, 16)),
    ((3, 16, 0, 48),),
)


class Sender:
    def __init__(self, send_sem, recv_sem):
        self.sems = (send_sem, recv_sem)
        self.started = []

    def __call__(self, src, dst, peer):
        n = len(self.started)
        copy = pltpu.make_async_remote_copy(
            src, dst, self.sems[0].at[n], self.sems[1].at[n],
            device_id=peer, device_id_type=MESH,
        )
        copy.start()
        self.started.append(copy)
        return copy

    def finish(self):
        for copy in self.started:
            copy.wait_send()


def landed(copies):
    for copy in copies:
        copy.wait_recv()


def back_kernel(
    mix_ref, dgate_ref, dupper_ref, hidden_ref, input_ref, cotangent_ref,
    got_ref, out_ref,
    gate_ref, up_ref, down_ref, wgot, xsend, xgot,
    send_sem, recv_sem, own_sem, line_send, line_recv,
):
    x, yh, z, yl, c = place()
    f32, bf16 = jnp.float32, jnp.bfloat16
    pair = device(x, yh, z, yl, 1 - c)
    xs = [device((x + k) % 4, yh, z, yl, c) for k in (1, 2, 3)]
    signal(xs)
    others = greet_line()
    send = Sender(send_sem, recv_sem)
    side = input_ref.shape[1]

    def product(a, b):
        dims = (((1,), (1,)), ((), ()))
        return lax.dot_general(a, b, dims, preferred_element_type=f32).astype(bf16)

    def multiply(core):
        for i in range(2):
            k = 2 * core + i
            gate_ref[k] = product(dgate_ref[k], input_ref[k])
            up_ref[k] = product(dupper_ref[k], input_ref[k])
            at = pl.ds(pl.multiple_of(k * side, 16), side)
            for n in range(4):
                down_ref[k, n * side : (n + 1) * side] = product(
                    hidden_ref[n, at, :], cotangent_ref[k]
                )

    multiply(1 - c)
    await_all(len(xs) + others)

    grads = (gate_ref, up_ref, down_ref)
    copies = [
        send(ref.at[pl.ds(2 * (1 - c), 2)], wgot.at[kind], pair)
        for kind, ref in enumerate(grads)
    ]
    exchange = Exchange(mix_ref, got_ref, own_sem, line_send, line_recv)
    exchange.start()
    multiply(c)
    for dest in range(4):
        for h in range(2):
            for q in range(4):
                xsend[dest, h * 4 + q, :, 96:128] = jnp.zeros((ROWS, 32), bf16)
            for q in (1, 3):
                xsend[dest, h * 4 + q, 64:ROWS] = jnp.zeros((ROWS - 64, 128), bf16)
    landed(copies)
    for dest in range(4):
        for h in range(2):
            first = (dest * 2 + h) * 48
            for i, pieces in enumerate(PIECES):
                kind, k = divmod(i, 2)
                for q, row, start, rows in pieces:
                    at = slice(first + start, first + start + rows)
                    total = grads[kind][2 * c + k, at, :].astype(f32)
                    total = total + wgot[kind, k, at, :].astype(f32)
                    xsend[dest, h * 4 + q, row : row + rows, 0:96] = total.astype(bf16)

    copies = [
        send(xsend.at[(x + k) % 4], xgot.at[k - 1], peer) for k, peer in zip((1, 2, 3), xs)
    ]
    exchange.wait()
    landed(copies)

    def add_x(n, carry):
        total = xsend[x, n].astype(f32)
        for k in range(3):
            total = total + xgot[k, n].astype(f32)
        out_ref[n] = total.astype(bf16)
        return carry

    lax.fori_loop(0, 8, add_x, 0)
    send.finish()


def exchange_back(mix, dgate, dupper, hidden, hidden_in, cotangent):
    vmem = pl.BlockSpec(memory_space=pltpu.VMEM)
    bf16 = jnp.bfloat16
    return pl.pallas_call(
        back_kernel,
        out_shape=(
            jax.ShapeDtypeStruct(mix.shape, mix.dtype),
            jax.ShapeDtypeStruct((8, ROWS, 128), bf16),
        ),
        in_specs=[vmem] * 6,
        out_specs=(vmem,) * 2,
        scratch_shapes=[
            pltpu.VMEM((4, 384, 96), bf16),
            pltpu.VMEM((4, 384, 96), bf16),
            pltpu.VMEM((4, 384, 96), bf16),
            pltpu.VMEM((3, 2, 384, 96), bf16),
            pltpu.VMEM((4, 8, ROWS, 128), bf16),
            pltpu.VMEM((3, 8, ROWS, 128), bf16),
            pltpu.SemaphoreType.DMA((6,)),
            pltpu.SemaphoreType.DMA((6,)),
        ]
        + line_semaphores(mix.shape[0]),
        compiler_params=pltpu.CompilerParams(collective_id=3, has_side_effects=True),
        name="exchange_back",
    )(mix, dgate, dupper, hidden, hidden_in, cotangent)


def sum_kernel(
    factor,
    part_ref, left_ref, right_ref, in_ref, outg_ref, norm_ref,
    out_ref,
    rep_ref, rgot, ysend, ygot, zall, yall, repall, wgot, wzall, wyall, wother,
    send_sem, recv_sem,
):
    x, yh, z, yl, c = place()
    f32, bf16 = jnp.float32, jnp.bfloat16
    y = yh * 4 + yl
    pair = device(x, yh, z, yl, 1 - c)
    xs = [device((x + k) % 4, yh, z, yl, c) for k in (1, 2, 3)]
    xo = [device((x + k) % 4, yh, z, yl, 1 - c) for k in (1, 2, 3)]
    near = [device(x, yh, z, (yl + k) % 4, c) for k in (1, 2, 3)]
    far = [device(x, 1 - yh, z, (yl + k) % 4, c) for k in (0, 1, 2, 3)]
    zs = [device(x, yh, (z + k) % 8, yl, c) for k in range(1, 8)]
    peers = [pair] + xs + xo + near + far + zs
    signal(peers)
    for k in range(4):
        for n in range(8):
            row, lane = (k % 2) * 128 + n * 16, (k // 2) * 128
            rep_ref[0, k, n] = left_ref[row : row + 16, lane : lane + 128].astype(bf16)
            rep_ref[1, k, n] = jnp.zeros((16, 128), bf16)
    for n in range(2):
        for j in range(2):
            at = slice(32 * j + 16 * n, 32 * j + 16 * n + 16)
            rep_ref[1, 0, n, :, 64 * j : 64 * j + 64] = right_ref[at, :].astype(bf16)
    gains = [
        ref[128 * t : 128 * t + 128].reshape(1, 128)
        for ref in (in_ref, outg_ref, norm_ref)
        for t in range(3)
    ]
    gains.append(jnp.zeros((7, 128), f32))
    rep_ref[1, 0, 2] = jnp.concatenate(gains, axis=0).astype(bf16)
    await_all(len(peers))
    send = Sender(send_sem, recv_sem)

    copies = [send(rep_ref.at[1 - c, x], rgot.at[0], pair)]
    for k in (1, 2, 3):
        copies.append(send(rep_ref.at[c, (x + k) % 4], rgot.at[k], xs[k - 1]))
        copies.append(send(rep_ref.at[1 - c, (x + k) % 4], rgot.at[3 + k], xo[k - 1]))

    def along_y(src, dst):
        sent = [
            send(src.at[yh * 4 + (yl + k) % 4], dst.at[k - 1], peer)
            for k, peer in zip((1, 2, 3), near)
        ]
        return sent + [
            send(src.at[(1 - yh) * 4 + (yl + k) % 4], dst.at[3 + k], peer)
            for k, peer in zip((0, 1, 2, 3), far)
        ]

    def add(first, others):
        total = first.astype(f32)
        for k in range(others.shape[0]):
            total = total + others[k].astype(f32)
        return total.astype(bf16)

    def add_all(parts):
        total = parts[0].astype(f32)
        for k in range(1, 8):
            total = total + parts[k].astype(f32)
        return total.astype(bf16)

    w_y = along_y(part_ref, wgot)
    landed(copies)
    ysend[...] = add(rep_ref[c, x], rgot)
    r_y = along_y(ysend, ygot)
    landed(w_y)
    wzall[z] = add(part_ref[y], wgot)
    w_z = [send(wzall.at[z], wzall.at[z], peer) for peer in zs]
    landed(r_y)
    zall[z] = add(ysend[y], ygot)
    r_z = [send(zall.at[z], zall.at[z], peer) for peer in zs]
    landed(r_z)
    yall[y] = add_all(zall)
    r_back = [send(yall.at[y], yall.at[y], peer) for peer in near + far]
    landed(w_z)
    wyall[yl] = add_all(wzall)
    w_back = [send(wyall.at[yl], wyall.at[yl], peer) for peer in near]
    landed(r_back)
    copies = [send(yall, repall.at[c, x], peer) for peer in [pair] + xs + xo]
    repall[c, x] = yall[...]
    landed(w_back)
    w_pair = send(wyall, wother, pair)

    def unpack(chunk, core):
        for i, pieces in enumerate(PIECES):
            kind, k = divmod(i, 2)
            for q, row, start, rows in pieces:
                at = pl.multiple_of(kind * 192 + (2 * core + k) * 48 + start, 16)
                value = chunk[q, row : row + rows, 0:96].astype(f32) * factor
                out_ref[pl.ds(at, rows), 256:352] = value

    unpack(wyall, c)
    landed([w_pair])
    unpack(wother, 1 - c)
    landed(copies)
    for k in range(4):
        for n in range(8):
            row, lane = (k % 2) * 128 + n * 16, (k // 2) * 128
            value = repall[0, k, n].astype(f32) * factor
            out_ref[row : row + 16, lane : lane + 128] = value
    for n in range(2):
        value = repall[1, 0, n].astype(f32) * factor
        out_ref[256 + n * 16 : 272 + n * 16, 0:64] = value[:, 0:64]
        out_ref[288 + n * 16 : 304 + n * 16, 0:64] = value[:, 64:128]
    value = repall[1, 0, 2].astype(f32) * factor
    for j in range(3):
        for t in range(3):
            row = value[3 * j + t : 3 * j + t + 1, :]
            out_ref[576 + j : 577 + j, t * 128 : t * 128 + 128] = row
    send.finish()


def sum_gradients(grads, factor):
    vmem = pl.BlockSpec(memory_space=pltpu.VMEM)
    bf16 = jnp.bfloat16
    copies = 7 * 7 + 3 + 1
    return pl.pallas_call(
        functools.partial(sum_kernel, factor),
        out_shape=jax.ShapeDtypeStruct((584, 384), jnp.float32),
        in_specs=[vmem] * len(grads),
        out_specs=vmem,
        scratch_shapes=[
            pltpu.VMEM((2, 4, 8, 16, 128), bf16),
            pltpu.VMEM((7, 8, 16, 128), bf16),
            pltpu.VMEM((8, 16, 128), bf16),
            pltpu.VMEM((7, 16, 128), bf16),
            pltpu.VMEM((8, 16, 128), bf16),
            pltpu.VMEM((8, 16, 128), bf16),
            pltpu.VMEM((2, 4, 8, 16, 128), bf16),
            pltpu.VMEM((7, ROWS, 128), bf16),
            pltpu.VMEM((8, ROWS, 128), bf16),
            pltpu.VMEM((4, ROWS, 128), bf16),
            pltpu.VMEM((4, ROWS, 128), bf16),
            pltpu.SemaphoreType.DMA((copies,)),
            pltpu.SemaphoreType.DMA((copies,)),
        ],
        compiler_params=pltpu.CompilerParams(collective_id=2, has_side_effects=True),
        name="sum_gradients",
    )(*grads)


def split_kernel(sums_ref, left, right, gain_in, gain_out, norm, gate, up, down):
    left[...] = sums_ref[0:256, 0:256]
    right[...] = sums_ref[256:320, 0:64]
    for j, ref in enumerate((gain_in, gain_out, norm)):
        for t in range(3):
            row = sums_ref[576 + j : 577 + j, 128 * t : 128 * t + 128]
            ref[128 * t : 128 * t + 128] = row.reshape(128)
    for j, ref in enumerate((gate, up, down)):
        for k in range(4):
            at = 192 * j + 48 * k
            ref[k] = sums_ref[at : at + 48, 256:352]


def split_sums(sums):
    vmem = pl.BlockSpec(memory_space=pltpu.VMEM)
    shapes = [(256, 256), (64, 64)] + [(384,)] * 3 + [(4, 48, 96)] * 3
    return pl.pallas_call(
        split_kernel,
        out_shape=[jax.ShapeDtypeStruct(shape, jnp.float32) for shape in shapes],
        in_specs=[vmem],
        out_specs=[vmem] * len(shapes),
        name="split_sums",
    )(sums)


def shards(
    points,
    cotangent,
    in_gain,
    out_gain,
    left_factor,
    right_factor,
    norm_gain,
    gate_weight,
    up_weight,
    down_weight,
):
    seq_count = lax.axis_size("seq")
    data_count = lax.axis_size("dp")
    row_count = points.shape[1]
    channels = points.shape[2]
    block_size = left_factor.shape[0]
    block_total = right_factor.shape[0]
    blocks = row_count // block_size
    shard_width = gate_weight.shape[2]
    nblocks, block_in = gate_weight.shape[:2]
    block_hidden = data_count * shard_width
    quarter = block_hidden // nblocks
    packed = jnp.concatenate([gate_weight, up_weight, down_weight], axis=0).transpose(0, 2, 1)
    inputs = points[0].astype(jnp.float32)
    scaled = (inputs * in_gain).astype(jnp.bfloat16).reshape(blocks, block_size, channels)
    first_mix = jnp.einsum(
        "pb,abc->apc", left_factor, scaled, preferred_element_type=jnp.float32
    ).astype(jnp.bfloat16)
    weights, received = gather_weights(
        packed, first_mix.reshape(seq_count, block_size // seq_count, channels)
    )
    gate_full, up_full, down_full = weights[0:4], weights[4:8], weights[8:12]
    down_grid = down_full.reshape(nblocks, nblocks, quarter, block_in)
    mixed = jnp.einsum("qa,apc->pqc", right_factor, received, preferred_element_type=jnp.float32)
    first_moved = received
    mixed = mixed.reshape(row_count, channels)
    residual = inputs + out_gain * mixed
    inv_rms = lax.rsqrt(jnp.mean(residual * residual, axis=-1, keepdims=True) + 1e-05)
    normed = residual * inv_rms
    hidden_in = (normed * norm_gain).astype(jnp.bfloat16).reshape(row_count, nblocks, block_in)
    gate_pre = jnp.einsum("rkd,kfd->rkf", hidden_in, gate_full, preferred_element_type=jnp.float32)
    up_pre = jnp.einsum("rkd,kfd->rkf", hidden_in, up_full, preferred_element_type=jnp.float32)
    sig_gate = jax.nn.sigmoid(gate_pre)
    act_gate = gate_pre * sig_gate
    hidden = (act_gate * up_pre).astype(jnp.bfloat16)
    hidden_grid = hidden.reshape(row_count, nblocks, nblocks, quarter)
    branch = jnp.einsum(
        "rkjf,jkfo->rjo", hidden_grid, down_grid, preferred_element_type=jnp.float32
    ).reshape(row_count, channels)
    layer_out = (residual + branch).astype(jnp.bfloat16)
    grad_grid = cotangent[0].reshape(row_count, nblocks, block_in)
    dhidden = jnp.einsum(
        "rjo,jkfo->rkjf", grad_grid, down_grid, preferred_element_type=jnp.float32
    ).reshape(row_count, nblocks, block_hidden)
    dgate = (dhidden * up_pre * sig_gate * (1.0 + gate_pre * (1.0 - sig_gate))).astype(jnp.bfloat16)
    dupper = (dhidden * act_gate).astype(jnp.bfloat16)
    dhid_in = jnp.einsum("rkf,kfd->rkd", dgate, gate_full, preferred_element_type=jnp.float32)
    dhid_in = (
        dhid_in + jnp.einsum("rkf,kfd->rkd", dupper, up_full, preferred_element_type=jnp.float32)
    ).reshape(row_count, channels)
    grad_norm = jnp.sum(dhid_in * normed, axis=0)
    scaled_grad = dhid_in * norm_gain
    dresid = cotangent[0].astype(jnp.float32) + inv_rms * (
        scaled_grad - normed * jnp.mean(scaled_grad * normed, axis=-1, keepdims=True)
    )
    grad_out = jnp.sum(dresid * mixed, axis=0)
    dmixed = (
        (dresid * out_gain)
        .astype(jnp.bfloat16)
        .reshape(block_size // seq_count, block_total, channels)
    )
    dfirst = jnp.einsum(
        "qa,pqc->apc", right_factor, dmixed, preferred_element_type=jnp.float32
    ).astype(jnp.bfloat16)
    grad_right = jnp.einsum("pqc,apc->qa", dmixed, first_moved, preferred_element_type=jnp.float32)
    received, partial = exchange_back(
        dfirst,
        dgate.transpose(1, 2, 0),
        dupper.transpose(1, 2, 0),
        hidden.transpose(1, 2, 0),
        hidden_in.transpose(1, 2, 0),
        grad_grid.transpose(1, 2, 0),
    )
    received = received.reshape(1, block_size, channels)
    dscaled = jnp.einsum("pb,apc->abc", left_factor, received, preferred_element_type=jnp.float32)
    grad_left = jnp.einsum("apc,abc->pb", received, scaled, preferred_element_type=jnp.float32)
    dscaled = dscaled.reshape(row_count, channels)
    grad_in = jnp.sum(dscaled * inputs, axis=0)
    grad_points = (dresid + dscaled * in_gain).astype(jnp.bfloat16)
    factor = float(data_count * row_count * seq_count) ** (-0.5)
    sums = sum_gradients(
        (
            partial,
            grad_left,
            grad_right,
            grad_in,
            grad_out,
            grad_norm,
        ),
        factor,
    )

    left_sum, right_sum, in_sum, out_sum, norm_sum, *w_sums = split_sums(sums)
    return (
        layer_out[None],
        grad_points[None],
        left_sum,
        right_sum,
        in_sum,
        out_sum,
        norm_sum,
        *(w_sum.transpose(0, 2, 1) for w_sum in w_sums),
    )


def solution(mesh):
    in_specs = (
        P("dp", "seq", None),
        P("dp", "seq", None),
        P(),
        P(),
        P(),
        P(),
        P(),
        P(None, None, "dp"),
        P(None, None, "dp"),
        P(None, None, "dp"),
    )
    out_specs = (
        P("dp", "seq", None),
        P("dp", "seq", None),
        P(),
        P(),
        P(),
        P(),
        P(),
        P(None, None, "dp"),
        P(None, None, "dp"),
        P(None, None, "dp"),
    )
    return jax.shard_map(shards, mesh=mesh, in_specs=in_specs, out_specs=out_specs, check_vma=False)
```

```python
import functools

import jax
import jax.numpy as jnp
from jax import lax
from jax.experimental import pallas as pl
from jax.experimental.pallas import tpu as pltpu
from jax.sharding import PartitionSpec as P

MESH = pl.DeviceIdType.MESH
ROWS = 80


def place():
    d = lax.axis_index("dp")
    s = lax.axis_index("seq")
    return d // 2, d % 2, s // 8, (s // 2) % 4, s % 2


def device(x, yh, z, yl, c):
    return (x * 2 + yh, (z * 4 + yl) * 2 + c)


def signal(peers):
    barrier = pltpu.get_barrier_semaphore()
    for peer in peers:
        pl.semaphore_signal(barrier, inc=1, device_id=peer, device_id_type=MESH)


def await_all(count):
    pl.semaphore_wait(pltpu.get_barrier_semaphore(), count)


def greet(peers, others=0):
    signal(peers)
    await_all(len(peers) + others)


def line():
    d, s, n = lax.axis_index("dp"), lax.axis_index("seq"), lax.axis_size("seq")
    return d, s, n


def greet_line():
    d, s, n = line()
    barrier = pltpu.get_barrier_semaphore()

    def one(k, carry):
        pl.semaphore_signal(
            barrier, inc=1, device_id=(d, (s + k) % n), device_id_type=MESH
        )
        return carry

    lax.fori_loop(1, n, one, 0)
    return n - 1


class Exchange:
    def __init__(self, src, dst, local_sem, send_sem, recv_sem):
        self.refs = (src, dst)
        self.sems = (send_sem, recv_sem)
        s = lax.axis_index("seq")
        self.local = pltpu.make_async_copy(src.at[s], dst.at[s], local_sem)

    def copy(self, k):
        d, s, n = line()
        peer = (s + k) % n
        return pltpu.make_async_remote_copy(
            self.refs[0].at[peer], self.refs[1].at[s],
            self.sems[0].at[k - 1], self.sems[1].at[k - 1],
            device_id=(d, peer), device_id_type=MESH,
        )

    def start(self):
        def one(k, carry):
            self.copy(k).start()
            return carry

        lax.fori_loop(1, line()[2], one, 0)
        self.local.start()

    def wait(self):
        def one(k, carry):
            self.copy(k).wait()
            return carry

        self.local.wait()
        lax.fori_loop(1, line()[2], one, 0)


def gather_kernel(
    w_ref, mix_ref, out_ref, got_ref,
    local_sem, send_sem, recv_sem, own_sem, line_send, line_recv,
):
    x, yh, z, yl, c = place()
    pair = device(x, yh, z, yl, 1 - c)
    xs = [device((x + k) % 4, yh, z, yl, c) for k in (1, 2, 3)]
    across = [device(x, 1 - yh, z, k, c) for k in range(4)]
    width = w_ref.shape[1]
    half = w_ref.shape[0] // 2

    def part(d):
        at = pl.ds(pl.multiple_of(d * width, 16), width)
        return out_ref.at[pl.ds(half * c, half), at, :]

    def remote(src, dst, sent, got, peer):
        return pltpu.make_async_remote_copy(
            src, dst, send_sem.at[sent], recv_sem.at[got], device_id=peer, device_id_type=MESH
        )

    greet(xs + across, greet_line())
    own = w_ref.at[pl.ds(half * c, half)]
    mine = part(x * 2 + yh)
    theirs = part(x * 2 + 1 - yh)
    end = (yl == 0) | (yl == 3)
    base = 2 - 2 * (yl // 3)
    over = [
        remote(own, mine, n, 0, device(x, 1 - yh, z, base + n, c)) for n in range(2)
    ]

    @pl.when(end)
    def _():
        for copy in over:
            copy.start()

    sends = [remote(own, mine, 2 + n, 1 + n, peer) for n, peer in enumerate(xs)]
    for copy in sends:
        copy.start()
    exchange = Exchange(mix_ref, got_ref, own_sem, line_send, line_recv)
    exchange.start()
    local = pltpu.make_async_copy(own, mine, local_sem)
    local.start()
    over[0].wait_recv()
    for n, peer in enumerate(xs):
        copy = remote(theirs, theirs, 5 + n, 4 + n, peer)
        copy.start()
        sends.append(copy)
    local.wait()
    for copy in sends:
        copy.wait_recv()
    whole = out_ref.at[pl.ds(half * c, half)]
    copy = remote(whole, whole, 8, 7, pair)
    copy.start()
    exchange.wait()
    copy.wait_recv()
    for copy in sends + [copy]:
        copy.wait_send()

    @pl.when(end)
    def _():
        for copy in over:
            copy.wait_send()


def line_semaphores(n):
    return [
        pltpu.SemaphoreType.DMA,
        pltpu.SemaphoreType.DMA((n - 1,)),
        pltpu.SemaphoreType.DMA((n - 1,)),
    ]


def gather_weights(w, mix):
    n, width, d = w.shape
    vmem = pl.BlockSpec(memory_space=pltpu.VMEM)
    return pl.pallas_call(
        gather_kernel,
        out_shape=(
            jax.ShapeDtypeStruct((n, 8 * width, d), w.dtype),
            jax.ShapeDtypeStruct(mix.shape, mix.dtype),
        ),
        in_specs=[vmem] * 2,
        out_specs=(vmem,) * 2,
        scratch_shapes=[
            pltpu.SemaphoreType.DMA,
            pltpu.SemaphoreType.DMA((9,)),
            pltpu.SemaphoreType.DMA((8,)),
        ]
        + line_semaphores(mix.shape[0]),
        compiler_params=pltpu.CompilerParams(
            collective_id=1, has_side_effects=True, vmem_limit_bytes=8 << 20
        ),
        name="gather_weights",
    )(w, mix)


PIECES = (
    ((0, 0, 0, 48),),
    ((0, 48, 0, 32), (1, 0, 32, 16)),
    ((1, 16, 0, 48),),
    ((2, 0, 0, 48),),
    ((2, 48, 0, 32), (3, 0, 32, 16)),
    ((3, 16, 0, 48),),
)


class Sender:
    def __init__(self, send_sem, recv_sem):
        self.sems = (send_sem, recv_sem)
        self.started = []

    def __call__(self, src, dst, peer):
        n = len(self.started)
        copy = pltpu.make_async_remote_copy(
            src, dst, self.sems[0].at[n], self.sems[1].at[n],
            device_id=peer, device_id_type=MESH,
        )
        copy.start()
        self.started.append(copy)
        return copy

    def finish(self):
        for copy in self.started:
            copy.wait_send()


def landed(copies):
    for copy in copies:
        copy.wait_recv()


def back_kernel(
    mix_ref, dgate_ref, dupper_ref, hidden_ref, input_ref, cotangent_ref,
    got_ref, out_ref,
    gate_ref, up_ref, down_ref, wgot, xsend, xgot,
    send_sem, recv_sem, own_sem, line_send, line_recv,
):
    x, yh, z, yl, c = place()
    f32, bf16 = jnp.float32, jnp.bfloat16
    pair = device(x, yh, z, yl, 1 - c)
    xs = [device((x + k) % 4, yh, z, yl, c) for k in (1, 2, 3)]
    signal(xs)
    others = greet_line()
    send = Sender(send_sem, recv_sem)
    side = input_ref.shape[1]

    def product(a, b):
        dims = (((1,), (1,)), ((), ()))
        return lax.dot_general(a, b, dims, preferred_element_type=f32).astype(bf16)

    def multiply(core):
        for i in range(2):
            k = 2 * core + i
            gate_ref[k] = product(dgate_ref[k], input_ref[k])
            up_ref[k] = product(dupper_ref[k], input_ref[k])
            at = pl.ds(pl.multiple_of(k * side, 16), side)
            for n in range(4):
                down_ref[k, n * side : (n + 1) * side] = product(
                    hidden_ref[n, at, :], cotangent_ref[k]
                )

    multiply(1 - c)
    await_all(len(xs) + others)

    grads = (gate_ref, up_ref, down_ref)
    copies = [
        send(ref.at[pl.ds(2 * (1 - c), 2)], wgot.at[kind], pair)
        for kind, ref in enumerate(grads)
    ]
    exchange = Exchange(mix_ref, got_ref, own_sem, line_send, line_recv)
    exchange.start()
    multiply(c)
    for dest in range(4):
        for h in range(2):
            for q in range(4):
                xsend[dest, h * 4 + q, :, 96:128] = jnp.zeros((ROWS, 32), bf16)
            for q in (1, 3):
                xsend[dest, h * 4 + q, 64:ROWS] = jnp.zeros((ROWS - 64, 128), bf16)
    landed(copies)
    for dest in range(4):
        for h in range(2):
            first = (dest * 2 + h) * 48
            for i, pieces in enumerate(PIECES):
                kind, k = divmod(i, 2)
                for q, row, start, rows in pieces:
                    at = slice(first + start, first + start + rows)
                    total = grads[kind][2 * c + k, at, :].astype(f32)
                    total = total + wgot[kind, k, at, :].astype(f32)
                    xsend[dest, h * 4 + q, row : row + rows, 0:96] = total.astype(bf16)

    copies = [
        send(xsend.at[(x + k) % 4], xgot.at[k - 1], peer) for k, peer in zip((1, 2, 3), xs)
    ]
    exchange.wait()
    landed(copies)

    def add_x(n, carry):
        total = xsend[x, n].astype(f32)
        for k in range(3):
            total = total + xgot[k, n].astype(f32)
        out_ref[n] = total.astype(bf16)
        return carry

    lax.fori_loop(0, 8, add_x, 0)
    send.finish()


def exchange_back(mix, dgate, dupper, hidden, hidden_in, cotangent):
    vmem = pl.BlockSpec(memory_space=pltpu.VMEM)
    bf16 = jnp.bfloat16
    return pl.pallas_call(
        back_kernel,
        out_shape=(
            jax.ShapeDtypeStruct(mix.shape, mix.dtype),
            jax.ShapeDtypeStruct((8, ROWS, 128), bf16),
        ),
        in_specs=[vmem] * 6,
        out_specs=(vmem,) * 2,
        scratch_shapes=[
            pltpu.VMEM((4, 384, 96), bf16),
            pltpu.VMEM((4, 384, 96), bf16),
            pltpu.VMEM((4, 384, 96), bf16),
            pltpu.VMEM((3, 2, 384, 96), bf16),
            pltpu.VMEM((4, 8, ROWS, 128), bf16),
            pltpu.VMEM((3, 8, ROWS, 128), bf16),
            pltpu.SemaphoreType.DMA((6,)),
            pltpu.SemaphoreType.DMA((6,)),
        ]
        + line_semaphores(mix.shape[0]),
        compiler_params=pltpu.CompilerParams(
            collective_id=3, has_side_effects=True, vmem_limit_bytes=16 << 20
        ),
        name="exchange_back",
    )(mix, dgate, dupper, hidden, hidden_in, cotangent)


def sum_kernel(
    factor,
    part_ref, left_ref, right_ref, in_ref, outg_ref, norm_ref,
    out_ref,
    rep_ref, rgot, ysend, ygot, zall, yall, repall, wgot, wzall, wyall, wother,
    send_sem, recv_sem,
):
    x, yh, z, yl, c = place()
    f32, bf16 = jnp.float32, jnp.bfloat16
    y = yh * 4 + yl
    pair = device(x, yh, z, yl, 1 - c)
    xs = [device((x + k) % 4, yh, z, yl, c) for k in (1, 2, 3)]
    xo = [device((x + k) % 4, yh, z, yl, 1 - c) for k in (1, 2, 3)]
    near = [device(x, yh, z, (yl + k) % 4, c) for k in (1, 2, 3)]
    far = [device(x, 1 - yh, z, (yl + k) % 4, c) for k in (0, 1, 2, 3)]
    zs = [device(x, yh, (z + k) % 8, yl, c) for k in range(1, 8)]
    peers = [pair] + xs + xo + near + far + zs
    signal(peers)
    for k in range(4):
        for n in range(8):
            row, lane = (k % 2) * 128 + n * 16, (k // 2) * 128
            rep_ref[0, k, n] = left_ref[row : row + 16, lane : lane + 128].astype(bf16)
            rep_ref[1, k, n] = jnp.zeros((16, 128), bf16)
    for n in range(2):
        for j in range(2):
            at = slice(32 * j + 16 * n, 32 * j + 16 * n + 16)
            rep_ref[1, 0, n, :, 64 * j : 64 * j + 64] = right_ref[at, :].astype(bf16)
    gains = [
        ref[128 * t : 128 * t + 128].reshape(1, 128)
        for ref in (in_ref, outg_ref, norm_ref)
        for t in range(3)
    ]
    gains.append(jnp.zeros((7, 128), f32))
    rep_ref[1, 0, 2] = jnp.concatenate(gains, axis=0).astype(bf16)
    await_all(len(peers))
    send = Sender(send_sem, recv_sem)

    copies = [send(rep_ref.at[1 - c, x], rgot.at[0], pair)]
    for k in (1, 2, 3):
        copies.append(send(rep_ref.at[c, (x + k) % 4], rgot.at[k], xs[k - 1]))
        copies.append(send(rep_ref.at[1 - c, (x + k) % 4], rgot.at[3 + k], xo[k - 1]))

    def along_y(src, dst):
        sent = [
            send(src.at[yh * 4 + (yl + k) % 4], dst.at[k - 1], peer)
            for k, peer in zip((1, 2, 3), near)
        ]
        return sent + [
            send(src.at[(1 - yh) * 4 + (yl + k) % 4], dst.at[3 + k], peer)
            for k, peer in zip((0, 1, 2, 3), far)
        ]

    def add(first, others):
        total = first.astype(f32)
        for k in range(others.shape[0]):
            total = total + others[k].astype(f32)
        return total.astype(bf16)

    def add_all(parts):
        total = parts[0].astype(f32)
        for k in range(1, 8):
            total = total + parts[k].astype(f32)
        return total.astype(bf16)

    w_y = along_y(part_ref, wgot)
    landed(copies)
    ysend[...] = add(rep_ref[c, x], rgot)
    r_y = along_y(ysend, ygot)
    landed(w_y)
    wzall[z] = add(part_ref[y], wgot)
    w_z = [send(wzall.at[z], wzall.at[z], peer) for peer in zs]
    landed(r_y)
    zall[z] = add(ysend[y], ygot)
    r_z = [send(zall.at[z], zall.at[z], peer) for peer in zs]
    landed(r_z)
    yall[y] = add_all(zall)
    r_back = [send(yall.at[y], yall.at[y], peer) for peer in near + far]
    landed(w_z)
    wyall[yl] = add_all(wzall)
    w_back = [send(wyall.at[yl], wyall.at[yl], peer) for peer in near]
    landed(r_back)
    copies = [send(yall, repall.at[c, x], peer) for peer in [pair] + xs + xo]
    repall[c, x] = yall[...]
    landed(w_back)
    w_pair = send(wyall, wother, pair)

    def unpack(chunk, core):
        for i, pieces in enumerate(PIECES):
            kind, k = divmod(i, 2)
            for q, row, start, rows in pieces:
                at = pl.multiple_of(kind * 192 + (2 * core + k) * 48 + start, 16)
                value = chunk[q, row : row + rows, 0:96].astype(f32) * factor
                out_ref[pl.ds(at, rows), 256:352] = value

    unpack(wyall, c)
    landed([w_pair])
    unpack(wother, 1 - c)
    landed(copies)
    for k in range(4):
        for n in range(8):
            row, lane = (k % 2) * 128 + n * 16, (k // 2) * 128
            value = repall[0, k, n].astype(f32) * factor
            out_ref[row : row + 16, lane : lane + 128] = value
    for n in range(2):
        value = repall[1, 0, n].astype(f32) * factor
        out_ref[256 + n * 16 : 272 + n * 16, 0:64] = value[:, 0:64]
        out_ref[288 + n * 16 : 304 + n * 16, 0:64] = value[:, 64:128]
    value = repall[1, 0, 2].astype(f32) * factor
    for j in range(3):
        for t in range(3):
            row = value[3 * j + t : 3 * j + t + 1, :]
            out_ref[576 + j : 577 + j, t * 128 : t * 128 + 128] = row
    send.finish()


def sum_gradients(grads, factor):
    vmem = pl.BlockSpec(memory_space=pltpu.VMEM)
    bf16 = jnp.bfloat16
    copies = 7 * 7 + 3 + 1
    return pl.pallas_call(
        functools.partial(sum_kernel, factor),
        out_shape=jax.ShapeDtypeStruct((584, 384), jnp.float32),
        in_specs=[vmem] * len(grads),
        out_specs=vmem,
        scratch_shapes=[
            pltpu.VMEM((2, 4, 8, 16, 128), bf16),
            pltpu.VMEM((7, 8, 16, 128), bf16),
            pltpu.VMEM((8, 16, 128), bf16),
            pltpu.VMEM((7, 16, 128), bf16),
            pltpu.VMEM((8, 16, 128), bf16),
            pltpu.VMEM((8, 16, 128), bf16),
            pltpu.VMEM((2, 4, 8, 16, 128), bf16),
            pltpu.VMEM((7, ROWS, 128), bf16),
            pltpu.VMEM((8, ROWS, 128), bf16),
            pltpu.VMEM((4, ROWS, 128), bf16),
            pltpu.VMEM((4, ROWS, 128), bf16),
            pltpu.SemaphoreType.DMA((copies,)),
            pltpu.SemaphoreType.DMA((copies,)),
        ],
        compiler_params=pltpu.CompilerParams(
            collective_id=2, has_side_effects=True, vmem_limit_bytes=8 << 20
        ),
        name="sum_gradients",
    )(*grads)


def split_kernel(sums_ref, left, right, gain_in, gain_out, norm, gate, up, down):
    left[...] = sums_ref[0:256, 0:256]
    right[...] = sums_ref[256:320, 0:64]
    for j, ref in enumerate((gain_in, gain_out, norm)):
        for t in range(3):
            row = sums_ref[576 + j : 577 + j, 128 * t : 128 * t + 128]
            ref[128 * t : 128 * t + 128] = row.reshape(128)
    for j, ref in enumerate((gate, up, down)):
        for k in range(4):
            at = 192 * j + 48 * k
            ref[k] = sums_ref[at : at + 48, 256:352]


def split_sums(sums):
    vmem = pl.BlockSpec(memory_space=pltpu.VMEM)
    shapes = [(256, 256), (64, 64)] + [(384,)] * 3 + [(4, 48, 96)] * 3
    return pl.pallas_call(
        split_kernel,
        out_shape=[jax.ShapeDtypeStruct(shape, jnp.float32) for shape in shapes],
        in_specs=[vmem],
        out_specs=[vmem] * len(shapes),
        compiler_params=pltpu.CompilerParams(vmem_limit_bytes=8 << 20),
        name="split_sums",
    )(sums)


def shards(
    points,
    cotangent,
    in_gain,
    out_gain,
    left_factor,
    right_factor,
    norm_gain,
    gate_weight,
    up_weight,
    down_weight,
):
    seq_count = lax.axis_size("seq")
    data_count = lax.axis_size("dp")
    row_count = points.shape[1]
    channels = points.shape[2]
    block_size = left_factor.shape[0]
    block_total = right_factor.shape[0]
    blocks = row_count // block_size
    shard_width = gate_weight.shape[2]
    nblocks, block_in = gate_weight.shape[:2]
    block_hidden = data_count * shard_width
    quarter = block_hidden // nblocks
    packed = jnp.concatenate([gate_weight, up_weight, down_weight], axis=0).transpose(0, 2, 1)
    inputs = points[0].astype(jnp.float32)
    scaled = (inputs * in_gain).astype(jnp.bfloat16).reshape(blocks, block_size, channels)
    first_mix = jnp.einsum(
        "pb,abc->apc", left_factor, scaled, preferred_element_type=jnp.float32
    ).astype(jnp.bfloat16)
    weights, received = gather_weights(
        packed, first_mix.reshape(seq_count, block_size // seq_count, channels)
    )
    gate_full, up_full, down_full = weights[0:4], weights[4:8], weights[8:12]
    down_grid = down_full.reshape(nblocks, nblocks, quarter, block_in)
    mixed = jnp.einsum("qa,apc->pqc", right_factor, received, preferred_element_type=jnp.float32)
    first_moved = received
    mixed = mixed.reshape(row_count, channels)
    residual = inputs + out_gain * mixed
    inv_rms = lax.rsqrt(jnp.mean(residual * residual, axis=-1, keepdims=True) + 1e-05)
    normed = residual * inv_rms
    hidden_in = (normed * norm_gain).astype(jnp.bfloat16).reshape(row_count, nblocks, block_in)
    gate_pre = jnp.einsum("rkd,kfd->rkf", hidden_in, gate_full, preferred_element_type=jnp.float32)
    up_pre = jnp.einsum("rkd,kfd->rkf", hidden_in, up_full, preferred_element_type=jnp.float32)
    sig_gate = jax.nn.sigmoid(gate_pre)
    act_gate = gate_pre * sig_gate
    hidden = (act_gate * up_pre).astype(jnp.bfloat16)
    hidden_grid = hidden.reshape(row_count, nblocks, nblocks, quarter)
    branch = jnp.einsum(
        "rkjf,jkfo->rjo", hidden_grid, down_grid, preferred_element_type=jnp.float32
    ).reshape(row_count, channels)
    layer_out = (residual + branch).astype(jnp.bfloat16)
    grad_grid = cotangent[0].reshape(row_count, nblocks, block_in)
    dhidden = jnp.einsum(
        "rjo,jkfo->rkjf", grad_grid, down_grid, preferred_element_type=jnp.float32
    ).reshape(row_count, nblocks, block_hidden)
    dgate = (dhidden * up_pre * sig_gate * (1.0 + gate_pre * (1.0 - sig_gate))).astype(jnp.bfloat16)
    dupper = (dhidden * act_gate).astype(jnp.bfloat16)
    dhid_in = jnp.einsum("rkf,kfd->rkd", dgate, gate_full, preferred_element_type=jnp.float32)
    dhid_in = (
        dhid_in + jnp.einsum("rkf,kfd->rkd", dupper, up_full, preferred_element_type=jnp.float32)
    ).reshape(row_count, channels)
    grad_norm = jnp.sum(dhid_in * normed, axis=0)
    scaled_grad = dhid_in * norm_gain
    dresid = cotangent[0].astype(jnp.float32) + inv_rms * (
        scaled_grad - normed * jnp.mean(scaled_grad * normed, axis=-1, keepdims=True)
    )
    grad_out = jnp.sum(dresid * mixed, axis=0)
    dmixed = (
        (dresid * out_gain)
        .astype(jnp.bfloat16)
        .reshape(block_size // seq_count, block_total, channels)
    )
    dfirst = jnp.einsum(
        "qa,pqc->apc", right_factor, dmixed, preferred_element_type=jnp.float32
    ).astype(jnp.bfloat16)
    grad_right = jnp.einsum("pqc,apc->qa", dmixed, first_moved, preferred_element_type=jnp.float32)
    received, partial = exchange_back(
        dfirst,
        dgate.transpose(1, 2, 0),
        dupper.transpose(1, 2, 0),
        hidden.transpose(1, 2, 0),
        hidden_in.transpose(1, 2, 0),
        grad_grid.transpose(1, 2, 0),
    )
    received = received.reshape(1, block_size, channels)
    dscaled = jnp.einsum("pb,apc->abc", left_factor, received, preferred_element_type=jnp.float32)
    grad_left = jnp.einsum("apc,abc->pb", received, scaled, preferred_element_type=jnp.float32)
    dscaled = dscaled.reshape(row_count, channels)
    grad_in = jnp.sum(dscaled * inputs, axis=0)
    grad_points = (dresid + dscaled * in_gain).astype(jnp.bfloat16)
    factor = float(data_count * row_count * seq_count) ** (-0.5)
    sums = sum_gradients(
        (
            partial,
            grad_left,
            grad_right,
            grad_in,
            grad_out,
            grad_norm,
        ),
        factor,
    )

    left_sum, right_sum, in_sum, out_sum, norm_sum, *w_sums = split_sums(sums)
    return (
        layer_out[None],
        grad_points[None],
        left_sum,
        right_sum,
        in_sum,
        out_sum,
        norm_sum,
        *(w_sum.transpose(0, 2, 1) for w_sum in w_sums),
    )


def solution(mesh):
    in_specs = (
        P("dp", "seq", None),
        P("dp", "seq", None),
        P(),
        P(),
        P(),
        P(),
        P(),
        P(None, None, "dp"),
        P(None, None, "dp"),
        P(None, None, "dp"),
    )
    out_specs = (
        P("dp", "seq", None),
        P("dp", "seq", None),
        P(),
        P(),
        P(),
        P(),
        P(),
        P(None, None, "dp"),
        P(None, None, "dp"),
        P(None, None, "dp"),
    )
    return jax.shard_map(shards, mesh=mesh, in_specs=in_specs, out_specs=out_specs, check_vma=False)
```

```python
import functools

import jax
import jax.numpy as jnp
from jax import lax
from jax.experimental import pallas as pl
from jax.experimental.pallas import tpu as pltpu
from jax.sharding import PartitionSpec as P

MESH = pl.DeviceIdType.MESH
ROWS = 80


def place():
    d = lax.axis_index("dp")
    s = lax.axis_index("seq")
    return d // 2, d % 2, s // 8, (s // 2) % 4, s % 2


def device(x, yh, z, yl, c):
    return (x * 2 + yh, (z * 4 + yl) * 2 + c)


def signal(peers):
    barrier = pltpu.get_barrier_semaphore()
    for peer in peers:
        pl.semaphore_signal(barrier, inc=1, device_id=peer, device_id_type=MESH)


def await_all(count):
    pl.semaphore_wait(pltpu.get_barrier_semaphore(), count)


def greet(peers, others=0):
    signal(peers)
    await_all(len(peers) + others)


def line():
    d, s, n = lax.axis_index("dp"), lax.axis_index("seq"), lax.axis_size("seq")
    return d, s, n


def greet_line():
    d, s, n = line()
    barrier = pltpu.get_barrier_semaphore()

    def one(k, carry):
        pl.semaphore_signal(
            barrier, inc=1, device_id=(d, (s + k) % n), device_id_type=MESH
        )
        return carry

    lax.fori_loop(1, n, one, 0)
    return n - 1


class Exchange:
    def __init__(self, src, dst, local_sem, send_sem, recv_sem):
        self.refs = (src, dst)
        self.sems = (send_sem, recv_sem)
        s = lax.axis_index("seq")
        self.local = pltpu.make_async_copy(src.at[s], dst.at[s], local_sem)

    def copy(self, k):
        d, s, n = line()
        peer = (s + k) % n
        return pltpu.make_async_remote_copy(
            self.refs[0].at[peer], self.refs[1].at[s],
            self.sems[0].at[k - 1], self.sems[1].at[k - 1],
            device_id=(d, peer), device_id_type=MESH,
        )

    def start(self):
        def one(k, carry):
            self.copy(k).start()
            return carry

        lax.fori_loop(1, line()[2], one, 0)
        self.local.start()

    def wait(self):
        def one(k, carry):
            self.copy(k).wait()
            return carry

        self.local.wait()
        lax.fori_loop(1, line()[2], one, 0)


def gather_kernel(
    w_ref, mix_ref, out_ref, got_ref,
    local_sem, send_sem, recv_sem, own_sem, line_send, line_recv,
):
    x, yh, z, yl, c = place()
    pair = device(x, yh, z, yl, 1 - c)
    xs = [device((x + k) % 4, yh, z, yl, c) for k in (1, 2, 3)]
    across = [device(x, 1 - yh, z, k, c) for k in range(4)]
    width = w_ref.shape[1]
    half = w_ref.shape[0] // 2

    def part(d):
        at = pl.ds(pl.multiple_of(d * width, 16), width)
        return out_ref.at[pl.ds(half * c, half), at, :]

    def remote(src, dst, sent, got, peer):
        return pltpu.make_async_remote_copy(
            src, dst, send_sem.at[sent], recv_sem.at[got], device_id=peer, device_id_type=MESH
        )

    greet(xs + across, greet_line())
    own = w_ref.at[pl.ds(half * c, half)]
    mine = part(x * 2 + yh)
    theirs = part(x * 2 + 1 - yh)
    end = (yl == 0) | (yl == 3)
    base = 2 - 2 * (yl // 3)
    over = [
        remote(own, mine, n, 0, device(x, 1 - yh, z, base + n, c)) for n in range(2)
    ]

    @pl.when(end)
    def _():
        for copy in over:
            copy.start()

    sends = [remote(own, mine, 2 + n, 1 + n, peer) for n, peer in enumerate(xs)]
    for copy in sends:
        copy.start()
    exchange = Exchange(mix_ref, got_ref, own_sem, line_send, line_recv)
    exchange.start()
    local = pltpu.make_async_copy(own, mine, local_sem)
    local.start()
    over[0].wait_recv()
    for n, peer in enumerate(xs):
        copy = remote(theirs, theirs, 5 + n, 4 + n, peer)
        copy.start()
        sends.append(copy)
    local.wait()
    swaps = []
    for first, h in ((0, yh), (3, 1 - yh)):
        for copy in sends[first : first + 3]:
            copy.wait_recv()
        for k in range(4):
            n = 4 * (first // 3) + k
            shard = part(2 * k + h)
            copy = remote(shard, shard, 8 + n, 7 + n, pair)
            copy.start()
            swaps.append(copy)
    exchange.wait()
    for copy in swaps:
        copy.wait_recv()
    for copy in sends + swaps:
        copy.wait_send()

    @pl.when(end)
    def _():
        for copy in over:
            copy.wait_send()


def line_semaphores(n):
    return [
        pltpu.SemaphoreType.DMA,
        pltpu.SemaphoreType.DMA((n - 1,)),
        pltpu.SemaphoreType.DMA((n - 1,)),
    ]


def gather_weights(w, mix):
    n, width, d = w.shape
    vmem = pl.BlockSpec(memory_space=pltpu.VMEM)
    return pl.pallas_call(
        gather_kernel,
        out_shape=(
            jax.ShapeDtypeStruct((n, 8 * width, d), w.dtype),
            jax.ShapeDtypeStruct(mix.shape, mix.dtype),
        ),
        in_specs=[vmem] * 2,
        out_specs=(vmem,) * 2,
        scratch_shapes=[
            pltpu.SemaphoreType.DMA,
            pltpu.SemaphoreType.DMA((16,)),
            pltpu.SemaphoreType.DMA((15,)),
        ]
        + line_semaphores(mix.shape[0]),
        compiler_params=pltpu.CompilerParams(
            collective_id=1, has_side_effects=True, vmem_limit_bytes=8 << 20
        ),
        name="gather_weights",
    )(w, mix)


PIECES = (
    ((0, 0, 0, 48),),
    ((0, 48, 0, 32), (1, 0, 32, 16)),
    ((1, 16, 0, 48),),
    ((2, 0, 0, 48),),
    ((2, 48, 0, 32), (3, 0, 32, 16)),
    ((3, 16, 0, 48),),
)


class Sender:
    def __init__(self, send_sem, recv_sem):
        self.sems = (send_sem, recv_sem)
        self.started = []

    def __call__(self, src, dst, peer):
        n = len(self.started)
        copy = pltpu.make_async_remote_copy(
            src, dst, self.sems[0].at[n], self.sems[1].at[n],
            device_id=peer, device_id_type=MESH,
        )
        copy.start()
        self.started.append(copy)
        return copy

    def finish(self):
        for copy in self.started:
            copy.wait_send()


def landed(copies):
    for copy in copies:
        copy.wait_recv()


def back_kernel(
    mix_ref, dgate_ref, dupper_ref, hidden_ref, input_ref, cotangent_ref,
    got_ref, out_ref,
    gate_ref, up_ref, down_ref, wgot, xsend, xgot,
    send_sem, recv_sem, own_sem, line_send, line_recv,
):
    x, yh, z, yl, c = place()
    f32, bf16 = jnp.float32, jnp.bfloat16
    pair = device(x, yh, z, yl, 1 - c)
    xs = [device((x + k) % 4, yh, z, yl, c) for k in (1, 2, 3)]
    signal(xs)
    others = greet_line()
    send = Sender(send_sem, recv_sem)
    side = input_ref.shape[1]

    def product(a, b):
        dims = (((1,), (1,)), ((), ()))
        return lax.dot_general(a, b, dims, preferred_element_type=f32).astype(bf16)

    def multiply(core):
        for i in range(2):
            k = 2 * core + i
            gate_ref[k] = product(dgate_ref[k], input_ref[k])
            up_ref[k] = product(dupper_ref[k], input_ref[k])
            at = pl.ds(pl.multiple_of(k * side, 16), side)
            for n in range(4):
                down_ref[k, n * side : (n + 1) * side] = product(
                    hidden_ref[n, at, :], cotangent_ref[k]
                )

    multiply(1 - c)
    await_all(len(xs) + others)

    grads = (gate_ref, up_ref, down_ref)
    copies = [
        send(ref.at[pl.ds(2 * (1 - c), 2)], wgot.at[kind], pair)
        for kind, ref in enumerate(grads)
    ]
    exchange = Exchange(mix_ref, got_ref, own_sem, line_send, line_recv)
    exchange.start()
    multiply(c)
    for dest in range(4):
        for h in range(2):
            for q in range(4):
                xsend[dest, h * 4 + q, :, 96:128] = jnp.zeros((ROWS, 32), bf16)
            for q in (1, 3):
                xsend[dest, h * 4 + q, 64:ROWS] = jnp.zeros((ROWS - 64, 128), bf16)
    landed(copies)
    for dest in range(4):
        for h in range(2):
            first = (dest * 2 + h) * 48
            for i, pieces in enumerate(PIECES):
                kind, k = divmod(i, 2)
                for q, row, start, rows in pieces:
                    at = slice(first + start, first + start + rows)
                    total = grads[kind][2 * c + k, at, :].astype(f32)
                    total = total + wgot[kind, k, at, :].astype(f32)
                    xsend[dest, h * 4 + q, row : row + rows, 0:96] = total.astype(bf16)

    copies = [
        send(xsend.at[(x + k) % 4], xgot.at[k - 1], peer) for k, peer in zip((1, 2, 3), xs)
    ]
    exchange.wait()
    landed(copies)

    def add_x(n, carry):
        total = xsend[x, n].astype(f32)
        for k in range(3):
            total = total + xgot[k, n].astype(f32)
        out_ref[n] = total.astype(bf16)
        return carry

    lax.fori_loop(0, 8, add_x, 0)
    send.finish()


def exchange_back(mix, dgate, dupper, hidden, hidden_in, cotangent):
    vmem = pl.BlockSpec(memory_space=pltpu.VMEM)
    bf16 = jnp.bfloat16
    return pl.pallas_call(
        back_kernel,
        out_shape=(
            jax.ShapeDtypeStruct(mix.shape, mix.dtype),
            jax.ShapeDtypeStruct((8, ROWS, 128), bf16),
        ),
        in_specs=[vmem] * 6,
        out_specs=(vmem,) * 2,
        scratch_shapes=[
            pltpu.VMEM((4, 384, 96), bf16),
            pltpu.VMEM((4, 384, 96), bf16),
            pltpu.VMEM((4, 384, 96), bf16),
            pltpu.VMEM((3, 2, 384, 96), bf16),
            pltpu.VMEM((4, 8, ROWS, 128), bf16),
            pltpu.VMEM((3, 8, ROWS, 128), bf16),
            pltpu.SemaphoreType.DMA((6,)),
            pltpu.SemaphoreType.DMA((6,)),
        ]
        + line_semaphores(mix.shape[0]),
        compiler_params=pltpu.CompilerParams(
            collective_id=3, has_side_effects=True, vmem_limit_bytes=16 << 20
        ),
        name="exchange_back",
    )(mix, dgate, dupper, hidden, hidden_in, cotangent)


def sum_kernel(
    factor,
    part_ref, left_ref, right_ref, in_ref, outg_ref, norm_ref,
    out_ref,
    rep_ref, rgot, ysend, ygot, zall, yall, repall, wgot, wzall, wyall, wother,
    send_sem, recv_sem,
):
    x, yh, z, yl, c = place()
    f32, bf16 = jnp.float32, jnp.bfloat16
    y = yh * 4 + yl
    pair = device(x, yh, z, yl, 1 - c)
    xs = [device((x + k) % 4, yh, z, yl, c) for k in (1, 2, 3)]
    xo = [device((x + k) % 4, yh, z, yl, 1 - c) for k in (1, 2, 3)]
    near = [device(x, yh, z, (yl + k) % 4, c) for k in (1, 2, 3)]
    far = [device(x, 1 - yh, z, (yl + k) % 4, c) for k in (0, 1, 2, 3)]
    zs = [device(x, yh, (z + k) % 8, yl, c) for k in range(1, 8)]
    peers = [pair] + xs + xo + near + far + zs
    signal(peers)
    for k in range(4):
        for n in range(8):
            row, lane = (k % 2) * 128 + n * 16, (k // 2) * 128
            rep_ref[0, k, n] = left_ref[row : row + 16, lane : lane + 128].astype(bf16)
            rep_ref[1, k, n] = jnp.zeros((16, 128), bf16)
    for n in range(2):
        for j in range(2):
            at = slice(32 * j + 16 * n, 32 * j + 16 * n + 16)
            rep_ref[1, 0, n, :, 64 * j : 64 * j + 64] = right_ref[at, :].astype(bf16)
    gains = [
        ref[128 * t : 128 * t + 128].reshape(1, 128)
        for ref in (in_ref, outg_ref, norm_ref)
        for t in range(3)
    ]
    gains.append(jnp.zeros((7, 128), f32))
    rep_ref[1, 0, 2] = jnp.concatenate(gains, axis=0).astype(bf16)
    await_all(len(peers))
    send = Sender(send_sem, recv_sem)

    copies = [send(rep_ref.at[1 - c, x], rgot.at[0], pair)]
    for k in (1, 2, 3):
        copies.append(send(rep_ref.at[c, (x + k) % 4], rgot.at[k], xs[k - 1]))
        copies.append(send(rep_ref.at[1 - c, (x + k) % 4], rgot.at[3 + k], xo[k - 1]))

    def along_y(src, dst):
        sent = [
            send(src.at[yh * 4 + (yl + k) % 4], dst.at[k - 1], peer)
            for k, peer in zip((1, 2, 3), near)
        ]
        return sent + [
            send(src.at[(1 - yh) * 4 + (yl + k) % 4], dst.at[3 + k], peer)
            for k, peer in zip((0, 1, 2, 3), far)
        ]

    def add(first, others):
        total = first.astype(f32)
        for k in range(others.shape[0]):
            total = total + others[k].astype(f32)
        return total.astype(bf16)

    def add_all(parts):
        total = parts[0].astype(f32)
        for k in range(1, 8):
            total = total + parts[k].astype(f32)
        return total.astype(bf16)

    w_y = along_y(part_ref, wgot)
    landed(copies)
    ysend[...] = add(rep_ref[c, x], rgot)
    r_y = along_y(ysend, ygot)
    landed(w_y)
    wzall[z] = add(part_ref[y], wgot)
    w_z = [send(wzall.at[z], wzall.at[z], peer) for peer in zs]
    landed(r_y)
    zall[z] = add(ysend[y], ygot)
    r_z = [send(zall.at[z], zall.at[z], peer) for peer in zs]
    landed(r_z)
    yall[y] = add_all(zall)
    r_back = [send(yall.at[y], yall.at[y], peer) for peer in near + far]
    landed(w_z)
    wyall[yl] = add_all(wzall)
    w_back = [send(wyall.at[yl], wyall.at[yl], peer) for peer in near]
    landed(r_back)
    copies = [send(yall, repall.at[c, x], peer) for peer in [pair] + xs + xo]
    repall[c, x] = yall[...]
    landed(w_back)
    w_pair = send(wyall, wother, pair)

    def unpack(chunk, core):
        for i, pieces in enumerate(PIECES):
            kind, k = divmod(i, 2)
            for q, row, start, rows in pieces:
                at = pl.multiple_of(kind * 192 + (2 * core + k) * 48 + start, 16)
                value = chunk[q, row : row + rows, 0:96].astype(f32) * factor
                out_ref[pl.ds(at, rows), 256:352] = value

    unpack(wyall, c)
    landed([w_pair])
    unpack(wother, 1 - c)
    landed(copies)
    for k in range(4):
        for n in range(8):
            row, lane = (k % 2) * 128 + n * 16, (k // 2) * 128
            value = repall[0, k, n].astype(f32) * factor
            out_ref[row : row + 16, lane : lane + 128] = value
    for n in range(2):
        value = repall[1, 0, n].astype(f32) * factor
        out_ref[256 + n * 16 : 272 + n * 16, 0:64] = value[:, 0:64]
        out_ref[288 + n * 16 : 304 + n * 16, 0:64] = value[:, 64:128]
    value = repall[1, 0, 2].astype(f32) * factor
    for j in range(3):
        for t in range(3):
            row = value[3 * j + t : 3 * j + t + 1, :]
            out_ref[576 + j : 577 + j, t * 128 : t * 128 + 128] = row
    send.finish()


def sum_gradients(grads, factor):
    vmem = pl.BlockSpec(memory_space=pltpu.VMEM)
    bf16 = jnp.bfloat16
    copies = 7 * 7 + 3 + 1
    return pl.pallas_call(
        functools.partial(sum_kernel, factor),
        out_shape=jax.ShapeDtypeStruct((584, 384), jnp.float32),
        in_specs=[vmem] * len(grads),
        out_specs=vmem,
        scratch_shapes=[
            pltpu.VMEM((2, 4, 8, 16, 128), bf16),
            pltpu.VMEM((7, 8, 16, 128), bf16),
            pltpu.VMEM((8, 16, 128), bf16),
            pltpu.VMEM((7, 16, 128), bf16),
            pltpu.VMEM((8, 16, 128), bf16),
            pltpu.VMEM((8, 16, 128), bf16),
            pltpu.VMEM((2, 4, 8, 16, 128), bf16),
            pltpu.VMEM((7, ROWS, 128), bf16),
            pltpu.VMEM((8, ROWS, 128), bf16),
            pltpu.VMEM((4, ROWS, 128), bf16),
            pltpu.VMEM((4, ROWS, 128), bf16),
            pltpu.SemaphoreType.DMA((copies,)),
            pltpu.SemaphoreType.DMA((copies,)),
        ],
        compiler_params=pltpu.CompilerParams(
            collective_id=2, has_side_effects=True, vmem_limit_bytes=8 << 20
        ),
        name="sum_gradients",
    )(*grads)


def split_kernel(sums_ref, left, right, gain_in, gain_out, norm, gate, up, down):
    left[...] = sums_ref[0:256, 0:256]
    right[...] = sums_ref[256:320, 0:64]
    for j, ref in enumerate((gain_in, gain_out, norm)):
        for t in range(3):
            row = sums_ref[576 + j : 577 + j, 128 * t : 128 * t + 128]
            ref[128 * t : 128 * t + 128] = row.reshape(128)
    for j, ref in enumerate((gate, up, down)):
        for k in range(4):
            at = 192 * j + 48 * k
            ref[k] = sums_ref[at : at + 48, 256:352]


def split_sums(sums):
    vmem = pl.BlockSpec(memory_space=pltpu.VMEM)
    shapes = [(256, 256), (64, 64)] + [(384,)] * 3 + [(4, 48, 96)] * 3
    return pl.pallas_call(
        split_kernel,
        out_shape=[jax.ShapeDtypeStruct(shape, jnp.float32) for shape in shapes],
        in_specs=[vmem],
        out_specs=[vmem] * len(shapes),
        compiler_params=pltpu.CompilerParams(vmem_limit_bytes=8 << 20),
        name="split_sums",
    )(sums)


def shards(
    points,
    cotangent,
    in_gain,
    out_gain,
    left_factor,
    right_factor,
    norm_gain,
    gate_weight,
    up_weight,
    down_weight,
):
    seq_count = lax.axis_size("seq")
    data_count = lax.axis_size("dp")
    row_count = points.shape[1]
    channels = points.shape[2]
    block_size = left_factor.shape[0]
    block_total = right_factor.shape[0]
    blocks = row_count // block_size
    shard_width = gate_weight.shape[2]
    nblocks, block_in = gate_weight.shape[:2]
    block_hidden = data_count * shard_width
    quarter = block_hidden // nblocks
    packed = jnp.concatenate([gate_weight, up_weight, down_weight], axis=0).transpose(0, 2, 1)
    inputs = points[0].astype(jnp.float32)
    scaled = (inputs * in_gain).astype(jnp.bfloat16).reshape(blocks, block_size, channels)
    first_mix = jnp.einsum(
        "pb,abc->apc", left_factor, scaled, preferred_element_type=jnp.float32
    ).astype(jnp.bfloat16)
    weights, received = gather_weights(
        packed, first_mix.reshape(seq_count, block_size // seq_count, channels)
    )
    gate_full, up_full, down_full = weights[0:4], weights[4:8], weights[8:12]
    down_grid = down_full.reshape(nblocks, nblocks, quarter, block_in)
    mixed = jnp.einsum("qa,apc->pqc", right_factor, received, preferred_element_type=jnp.float32)
    first_moved = received
    mixed = mixed.reshape(row_count, channels)
    residual = inputs + out_gain * mixed
    inv_rms = lax.rsqrt(jnp.mean(residual * residual, axis=-1, keepdims=True) + 1e-05)
    normed = residual * inv_rms
    hidden_in = (normed * norm_gain).astype(jnp.bfloat16).reshape(row_count, nblocks, block_in)
    gate_pre = jnp.einsum("rkd,kfd->rkf", hidden_in, gate_full, preferred_element_type=jnp.float32)
    up_pre = jnp.einsum("rkd,kfd->rkf", hidden_in, up_full, preferred_element_type=jnp.float32)
    sig_gate = jax.nn.sigmoid(gate_pre)
    act_gate = gate_pre * sig_gate
    hidden = (act_gate * up_pre).astype(jnp.bfloat16)
    hidden_grid = hidden.reshape(row_count, nblocks, nblocks, quarter)
    branch = jnp.einsum(
        "rkjf,jkfo->rjo", hidden_grid, down_grid, preferred_element_type=jnp.float32
    ).reshape(row_count, channels)
    layer_out = (residual + branch).astype(jnp.bfloat16)
    grad_grid = cotangent[0].reshape(row_count, nblocks, block_in)
    dhidden = jnp.einsum(
        "rjo,jkfo->rkjf", grad_grid, down_grid, preferred_element_type=jnp.float32
    ).reshape(row_count, nblocks, block_hidden)
    dgate = (dhidden * up_pre * sig_gate * (1.0 + gate_pre * (1.0 - sig_gate))).astype(jnp.bfloat16)
    dupper = (dhidden * act_gate).astype(jnp.bfloat16)
    dhid_in = jnp.einsum("rkf,kfd->rkd", dgate, gate_full, preferred_element_type=jnp.float32)
    dhid_in = (
        dhid_in + jnp.einsum("rkf,kfd->rkd", dupper, up_full, preferred_element_type=jnp.float32)
    ).reshape(row_count, channels)
    grad_norm = jnp.sum(dhid_in * normed, axis=0)
    scaled_grad = dhid_in * norm_gain
    dresid = cotangent[0].astype(jnp.float32) + inv_rms * (
        scaled_grad - normed * jnp.mean(scaled_grad * normed, axis=-1, keepdims=True)
    )
    grad_out = jnp.sum(dresid * mixed, axis=0)
    dmixed = (
        (dresid * out_gain)
        .astype(jnp.bfloat16)
        .reshape(block_size // seq_count, block_total, channels)
    )
    dfirst = jnp.einsum(
        "qa,pqc->apc", right_factor, dmixed, preferred_element_type=jnp.float32
    ).astype(jnp.bfloat16)
    grad_right = jnp.einsum("pqc,apc->qa", dmixed, first_moved, preferred_element_type=jnp.float32)
    received, partial = exchange_back(
        dfirst,
        dgate.transpose(1, 2, 0),
        dupper.transpose(1, 2, 0),
        hidden.transpose(1, 2, 0),
        hidden_in.transpose(1, 2, 0),
        grad_grid.transpose(1, 2, 0),
    )
    received = received.reshape(1, block_size, channels)
    dscaled = jnp.einsum("pb,apc->abc", left_factor, received, preferred_element_type=jnp.float32)
    grad_left = jnp.einsum("apc,abc->pb", received, scaled, preferred_element_type=jnp.float32)
    dscaled = dscaled.reshape(row_count, channels)
    grad_in = jnp.sum(dscaled * inputs, axis=0)
    grad_points = (dresid + dscaled * in_gain).astype(jnp.bfloat16)
    factor = float(data_count * row_count * seq_count) ** (-0.5)
    sums = sum_gradients(
        (
            partial,
            grad_left,
            grad_right,
            grad_in,
            grad_out,
            grad_norm,
        ),
        factor,
    )

    left_sum, right_sum, in_sum, out_sum, norm_sum, *w_sums = split_sums(sums)
    return (
        layer_out[None],
        grad_points[None],
        left_sum,
        right_sum,
        in_sum,
        out_sum,
        norm_sum,
        *(w_sum.transpose(0, 2, 1) for w_sum in w_sums),
    )


def solution(mesh):
    in_specs = (
        P("dp", "seq", None),
        P("dp", "seq", None),
        P(),
        P(),
        P(),
        P(),
        P(),
        P(None, None, "dp"),
        P(None, None, "dp"),
        P(None, None, "dp"),
    )
    out_specs = (
        P("dp", "seq", None),
        P("dp", "seq", None),
        P(),
        P(),
        P(),
        P(),
        P(),
        P(None, None, "dp"),
        P(None, None, "dp"),
        P(None, None, "dp"),
    )
    return jax.shard_map(shards, mesh=mesh, in_specs=in_specs, out_specs=out_specs, check_vma=False)
```
